256 devices in a mesh: row: 16 (over y, z_lo, core), col: 16 (over z_hi, x).
Axes of the slice: x: 4, y: 4, z: 8 (z_hi: 4, z_lo: 2; z = z_hi * 2 + z_lo), core: 2. Of those that a mesh axis runs over, the one named last changes fastest.
Arguments:
- features: bfloat16 [131072, 256], P(('row', 'col')), may hold values from -6 to 6
- w_self: bfloat16 [256, 256], replicated, may hold values from -0.375 to 0.375
- w_neigh: bfloat16 [256, 256], replicated, may hold values from -3 to 3
- cotangent: bfloat16 [131072, 256], P(('row', 'col')), may hold values from -6 to 6
- degree: int32 [131072], P(('row', 'col')), may hold values from 64 to 256
- tile_rows: int32 [65536], P(('row', 'col')), may hold values from 0 to 63
- tile_cols: int32 [65536], P(('row', 'col')), may hold values from 0 to 63
- tile_edges: int32 [4, 65536, 128], P(None, ('row', 'col')), may hold values from 0 to 127
- tile_count: int32 [256], P(('row', 'col')), may hold values from 4 to 256, as said below
Outputs:
- activations: bfloat16 [131072, 256], P(('row', 'col'))
- feature_grad: bfloat16 [131072, 256], P(('row', 'col'))
- grad_self: float32 [256, 256], replicated
- grad_neigh: float32 [256, 256], replicated
The draws below stay inside these ranges and needn't reach their ends.
Inputs may be any that keep to these rules, and one draw needn't show every extreme that they name: The busiest device uses all 256 of its slots; slots from tile_count on are ignored.
All inputs are finite; a program needn't handle non-finite values.
Results may differ from the reference program's by a relative error of at most 0.0059.
Values may be sent and summed in bfloat16 or wider, within the bound.
No kernel may reach another device: no remote copies, remote signals or barrier semaphores. Data moves between devices by JAX's collectives and lax.ppermute only.
A program may use at most 64 MiB of HBM per device.

```python
import math
import jax
import jax.numpy as jnp
import numpy as np
from jax import lax

F = 256
TILE = 128
EDGE_K = 4
TPD = 4
CAP = 256
ROWT = 64
COLT = 64
NODES = 131072
TILES = 65536
N_ROW = 16
N_COL = 16


def draw_tile_count(key, part):
    weights = jax.random.randint(key, (N_ROW * N_COL,), 1, 9)
    weights = weights * weights
    largest = jnp.max(weights)
    return (weights * CAP // largest).astype(jnp.int32)


def set_ends(entries, stream_key, smallest, high):
    shape = entries.shape
    place = [jax.random.randint(jax.random.fold_in(stream_key, axis), (), 0, shape[axis]) for axis in range(len(shape))]
    entries = entries.at[tuple(place)].set(smallest)
    longest = shape.index(max(shape))
    place[longest] = (place[longest] + 1) % shape[longest]
    return entries.at[tuple(place)].set(high)


def block_scale(stream_key, dims, split, smallest, high):
    def one(position, blocks):
        heights = jax.random.uniform(jax.random.fold_in(jax.random.fold_in(stream_key, 6), position), (blocks,), jnp.float32, smallest / len(split), high / len(split))
        return jnp.repeat(jnp.exp(heights), dims[position] // blocks).reshape((-1,) + (1,) * (len(dims) - position - 1))

    gain = one(*split[0])
    for cut in split[1:]:
        gain = gain * one(*cut)
    return gain


def rank_bounds(amount, skew):
    weights = [(1 << 20) // math.isqrt(grade ** skew) + 1 for grade in range(1, amount + 1)]
    scale = 1 + sum(weights) // (1 << 30)
    return np.cumsum(np.array([max(1, weight // scale) for weight in weights]))


def ranked(rng, dims, count, skew):
    table = rank_bounds(count, skew)
    pick = jax.random.randint(jax.random.fold_in(rng, 1), dims, 0, int(table[count - 1]))
    grade = jnp.searchsorted(jnp.asarray(table, jnp.int32), pick, side="right")
    return jax.random.permutation(jax.random.fold_in(rng, 2), count)[grade].astype(jnp.int32)


def normal_values(rng, extent, deviation, reach, shards=(), kind=jnp.bfloat16):
    entries = jax.random.normal(rng, extent, jnp.float32) * deviation
    if len(shards) > 0:
        entries = block_scale(rng, extent, shards, -0.22, 0.18) * entries
    return jnp.clip(entries, min=-reach, max=reach).astype(kind)


def setup_inputs(seed: int = 0) -> dict:
    splits = jax.random.split(jax.random.key(seed), 10)
    return {
        "features": normal_values(splits[0], (NODES, F), 1.0, 6.0, ((0, 256),)),
        "w_self": normal_values(splits[1], (F, F), F ** -0.5, 0.375),
        "w_neigh": normal_values(splits[2], (F, F), (max(F // 64, 1)) ** -0.5, 3.0),
        "cotangent": normal_values(splits[3], (NODES, F), 1.0, 6.0, ((0, 256),)),
        "degree": set_ends(jax.random.randint(splits[4], (NODES,), CAP * EDGE_K // (4 * TPD), CAP * EDGE_K // TPD + 1), jax.random.fold_in(splits[4], 1), CAP * EDGE_K // (4 * TPD), (CAP * EDGE_K // TPD + 1) - 1).astype(jnp.int32),
        "tile_rows": set_ends(ranked(splits[5], (TILES,), ROWT, 2), jax.random.fold_in(splits[5], 3), 0, ROWT - 1).astype(jnp.int32),
        "tile_cols": set_ends(jax.random.randint(splits[6], (TILES,), 0, COLT), jax.random.fold_in(splits[6], 1), 0, COLT - 1).astype(jnp.int32),
        "tile_edges": set_ends(jax.random.randint(splits[7], (EDGE_K, TILES, TILE), 0, TILE), jax.random.fold_in(splits[7], 1), 0, TILE - 1).astype(jnp.int32),
        "tile_count": draw_tile_count(jax.random.fold_in(splits[9], 71), 0),
    }


def device_edges(device, tile_rows, tile_cols, tile_edges, tile_count):
    row_index = device // N_COL
    col_index = device % N_COL
    first_slot = (device * CAP).astype(jnp.int32)
    slot_rows = lax.dynamic_slice_in_dim(tile_rows, first_slot, CAP)
    slot_cols = lax.dynamic_slice_in_dim(tile_cols, first_slot, CAP)
    slot_edges = lax.dynamic_slice_in_dim(tile_edges, first_slot, CAP, axis=1)
    in_use = (jnp.arange(CAP, dtype=jnp.int32) < tile_count[device]).astype(jnp.float32)
    global_rows = row_index * (N_COL * TPD) + slot_rows
    global_cols = (slot_cols // TPD * N_COL + col_index) * TPD + slot_cols % TPD
    offsets = jnp.arange(TILE, dtype=jnp.int32)
    targets = global_rows[:, None] * TILE + offsets[None, :]
    sources = global_cols[None, :, None] * TILE + slot_edges
    return (targets, sources, in_use)

def reference(features, w_self, w_neigh, cotangent, degree, tile_rows, tile_cols, tile_edges, tile_count):
    devices_all = jnp.arange(N_ROW * N_COL, dtype=jnp.int32)
    feats_wide = features.astype(jnp.float32)

    def gather_step(running, device):
        targets, sources, in_use = device_edges(device, tile_rows, tile_cols, tile_edges, tile_count)
        message = lax.optimization_barrier(jnp.sum(feats_wide[sources], axis=0)) * in_use[:, None, None]
        return (running.at[targets.reshape(-1)].add(message.reshape(-1, F)), None)
    neighbour_sum, _ = lax.scan(gather_step, jnp.zeros((NODES, F), jnp.float32), devices_all)
    degree_wide = degree.astype(jnp.float32)[:, None]
    aggregate = (neighbour_sum / degree_wide).astype(jnp.bfloat16)
    preact = jnp.dot(features, w_self, preferred_element_type=jnp.float32) + jnp.dot(aggregate, w_neigh, preferred_element_type=jnp.float32)
    sigmoid_pre = jax.nn.sigmoid(preact)
    activations = (preact * sigmoid_pre).astype(jnp.bfloat16)
    slope = sigmoid_pre * (1.0 + preact * (1.0 - sigmoid_pre))
    dpreact = (cotangent.astype(jnp.float32) * slope).astype(jnp.bfloat16)
    grad_scale = 1.0 / math.sqrt(NODES)
    grad_self = jnp.dot(features.T, dpreact, preferred_element_type=jnp.float32) * grad_scale
    grad_neigh = jnp.dot(aggregate.T, dpreact, preferred_element_type=jnp.float32) * grad_scale
    dscaled = (jnp.dot(dpreact, w_neigh.T, preferred_element_type=jnp.float32) / degree_wide).astype(jnp.bfloat16)
    dscaled_wide = dscaled.astype(jnp.float32)

    def spread_step(running, device):
        targets, sources, in_use = device_edges(device, tile_rows, tile_cols, tile_edges, tile_count)
        update = dscaled_wide[targets] * in_use[:, None, None]
        flat_update = update.reshape(-1, F)
        for edge_number in range(EDGE_K):
            running = running.at[sources[edge_number].reshape(-1)].add(flat_update)
        return (running, None)
    neighbour_grad, _ = lax.scan(spread_step, jnp.zeros((NODES, F), jnp.float32), devices_all)
    feature_grad = (jnp.dot(dpreact, w_self.T, preferred_element_type=jnp.float32) + neighbour_grad).astype(jnp.bfloat16)
    return (activations, feature_grad, grad_self, grad_neigh)
```

```python
import functools
import math

import jax
import jax.numpy as jnp
from jax import lax
from jax.experimental import pallas as pl
from jax.experimental.pallas import tpu as pltpu
from jax.sharding import PartitionSpec as P

F32, BF16, I32 = jnp.float32, jnp.bfloat16, jnp.int32
ROW, COL = "row", "col"
UNROLL = 8
BLOCK = 32
VMEM_LIMIT = 56 << 20


def shift_x(k):
    return [(4 * z + x, 4 * z + (x + k) % 4) for z in range(4) for x in range(4)]


def shift_z(k):
    return [(4 * z + x, 4 * ((z + k) % 4) + x) for z in range(4) for x in range(4)]


def shift_y(k):
    return [(4 * y + i, 4 * ((y + k) % 4) + i) for y in range(4) for i in range(4)]


SWAP_Z = [(i, i ^ 2) for i in range(16)]
SWAP_CORE = [(i, i ^ 1) for i in range(16)]


def list_kernel(pos, count, rows, cols, fslot, fsrc, fdst, bslot, bsrc, bdst, counts):
    room = fslot.shape[0]

    def clear(i, _):
        fslot[i] = 0
        fsrc[i] = 0
        fdst[i] = 32
        bslot[i] = 0
        bsrc[i] = 0
        bdst[i] = 32
        return 0

    lax.fori_loop(0, room, clear, 0)
    x, z, y, zl, core = pos[0], pos[1], pos[2], pos[3], pos[4]

    def place(s, held):
        f0, f1, b0, b1 = held
        row, col = rows[s], cols[s]
        tile, chunk = row & 1, (row >> 1) & 1
        rx, rz = (row >> 2) & 3, row >> 4
        ccore, czl, cy = (col >> 2) & 1, (col >> 3) & 1, col >> 4
        other = ccore ^ core
        half = (czl ^ zl) * 4 + (col & 3)
        fp = jnp.where(chunk == 0, f0, room - 1 - f1)
        fslot[fp] = s
        fsrc[fp] = other * 32 + ((y - cy) & 3) * 8 + half
        fdst[fp] = ((rx - x) & 3) * 8 + ((rz - z) & 3) * 2 + tile
        bp = jnp.where(other == 0, b0, room - 1 - b1)
        bslot[bp] = s
        bsrc[bp] = chunk * 32 + ((x - rx) & 3) * 8 + ((z - rz) & 3) * 2 + tile
        bdst[bp] = ((cy - y) & 3) * 8 + half
        return (f0 + 1 - chunk, f1 + chunk, b0 + 1 - other, b1 + other)

    zero = jnp.int32(0)
    held = lax.fori_loop(0, count[0], place, (zero, zero, zero, zero))
    for i in range(4):
        counts[i] = held[i]


def make_lists(pos, count, rows, cols, room):
    smem = pl.BlockSpec(memory_space=pltpu.SMEM)
    return pl.pallas_call(
        list_kernel,
        out_shape=[jax.ShapeDtypeStruct((room,), I32)] * 6 + [jax.ShapeDtypeStruct((8,), I32)],
        in_specs=[smem] * 4,
        out_specs=[smem] * 7,
        name="slot_lists",
    )(pos, count, rows, cols)


def mask_kernel(flip, slots, edges, out):
    base = pl.program_id(0) * BLOCK
    tile = out.shape[1]
    column = lax.broadcasted_iota(I32, (tile, tile), 0)
    edge_count = edges.shape[0]

    def one(i, _):
        s = slots[base + i]
        total = jnp.zeros((tile, tile), F32)
        for k in range(edge_count):
            total += jnp.where(edges[k, pl.ds(s, 1), :] == column, 1.0, 0.0)
        out[i] = (total.T if flip else total).astype(BF16)
        return 0

    lax.fori_loop(0, BLOCK, one, 0, unroll=4)


def make_masks(flip, slots, edges):
    room, tile = slots.shape[0], edges.shape[2]
    return pl.pallas_call(
        functools.partial(mask_kernel, flip),
        grid=(room // BLOCK,),
        out_shape=jax.ShapeDtypeStruct((room, tile, tile), BF16),
        in_specs=[
            pl.BlockSpec(memory_space=pltpu.SMEM),
            pl.BlockSpec(edges.shape, lambda i: (0, 0, 0)),
        ],
        out_specs=pl.BlockSpec((BLOCK, tile, tile), lambda i: (i, 0, 0)),
        cost_estimate=pl.CostEstimate(
            flops=room * tile * tile * 12, bytes_accessed=room * tile * tile * 2, transcendentals=0
        ),
        name="one_hot_tiles",
    )(slots, edges)


def product_kernel(side, n_in, n_out, counts, src, dst, masks, *refs):
    ins, outs = refs[:n_in], refs[n_in : n_in + n_out]
    held, tiles, total, staged, in_sems, tile_sems, out_sems = refs[n_in + n_out :]
    room, tile = masks.shape[0], masks.shape[1]
    n = counts[side]
    copies, at = [], 0
    for i, ref in enumerate(ins):
        size = ref.shape[0]
        copies.append(pltpu.make_async_copy(ref, held.at[pl.ds(at, size)], in_sems.at[i]))
        at += size
    blocks = (room - BLOCK) // BLOCK

    def block_copy(k):
        first = (k if side % 2 == 0 else room // BLOCK - 1 - k) * BLOCK
        part = pl.ds(first, BLOCK)
        return pltpu.make_async_copy(masks.at[part], tiles.at[part], tile_sems.at[k])

    for copy in copies:
        copy.start()
    for k in range(blocks):
        pl.when(n > k * BLOCK)(lambda k=k: block_copy(k).start())
    n_total = total.shape[0] - 1

    def clear(i, _):
        total[i] = jnp.zeros(total.shape[1:], F32)
        return 0

    lax.fori_loop(0, n_total, clear, 0)
    for copy in copies:
        copy.wait()
    for k in range(blocks):
        pl.when(n > k * BLOCK)(lambda k=k: block_copy(k).wait())
    steps = (n + UNROLL - 1) // UNROLL
    low = 0 if side % 2 == 0 else room - steps * UNROLL

    def step(i, _):
        first = low + i * UNROLL
        for half in range(0, UNROLL, 4):
            parts = [
                jnp.dot(
                    tiles[first + u],
                    held[pl.ds(pl.multiple_of(src[first + u] * tile, tile), tile), :],
                    preferred_element_type=F32,
                )
                for u in range(half, half + 4)
            ]
            for u in range(4):
                total[dst[first + half + u]] += parts[u]
        return 0

    lax.fori_loop(0, steps, step, 0)
    per = n_total // n_out
    sends = []
    for o, ref in enumerate(outs):

        def convert(i, _, o=o):
            j = o * per + i
            staged[pl.ds(pl.multiple_of(j * tile, tile), tile), :] = total[j].astype(BF16)
            return 0

        lax.fori_loop(0, per, convert, 0)
        rows = per * tile
        sends.append(pltpu.make_async_copy(staged.at[pl.ds(o * rows, rows)], ref, out_sems.at[o]))
        sends[-1].start()
    for send in sends:
        send.wait()


def products(side, n_out, counts, src, dst, masks, pieces):
    tile, width = masks.shape[1], pieces[0].shape[1]
    n_in, rows = len(pieces), sum(p.shape[0] for p in pieces)
    smem, anywhere = pl.BlockSpec(memory_space=pltpu.SMEM), pl.BlockSpec(memory_space=pl.ANY)
    return pl.pallas_call(
        functools.partial(product_kernel, side, n_in, n_out),
        out_shape=[jax.ShapeDtypeStruct((32 * tile // n_out, width), BF16)] * n_out,
        in_specs=[smem] * 3 + [anywhere] * (1 + n_in),
        out_specs=[anywhere] * n_out,
        scratch_shapes=[
            pltpu.VMEM((rows, width), BF16),
            pltpu.VMEM(masks.shape, BF16),
            pltpu.VMEM((33, tile, width), F32),
            pltpu.VMEM((32 * tile, width), BF16),
            pltpu.SemaphoreType.DMA((n_in,)),
            pltpu.SemaphoreType.DMA((masks.shape[0] // BLOCK,)),
            pltpu.SemaphoreType.DMA((n_out,)),
        ],
        compiler_params=pltpu.CompilerParams(vmem_limit_bytes=VMEM_LIMIT),
        cost_estimate=pl.CostEstimate(
            flops=128 * tile * tile * width * 2 * 4, bytes_accessed=12 << 20, transcendentals=0
        ),
        name="tile_products",
    )(counts, src, dst, masks, *pieces)


def spread(value, axis, shift):
    return [lax.ppermute(value, axis, shift(k)) for k in (1, 2, 3)]


def exchange(pieces, axis, shift):
    return [pieces[0]] + [lax.ppermute(pieces[k], axis, shift(k)) for k in (1, 2, 3)]


def add_up(parts):
    total = parts[0].astype(F32)
    for part in parts[1:]:
        total = total + part.astype(F32)
    return total


def scatter_sum(value, index, axis, shift):
    size = value.shape[0] // 4
    pieces = [lax.dynamic_slice_in_dim(value, ((index + k) & 3) * size, size) for k in range(4)]
    return add_up(exchange(pieces, axis, shift))


def gather_back(value, index, axis, shift):
    size = value.shape[0]
    full = jnp.zeros((4 * size, value.shape[1]), value.dtype)
    for k, piece in enumerate([value] + spread(value, axis, shift)):
        full = lax.dynamic_update_slice_in_dim(full, piece, ((index - k) & 3) * size, 0)
    return full


def sum_weights(grads, x, z, y):
    part = scatter_sum(grads, y, ROW, shift_y)
    part = scatter_sum(part, x, COL, shift_x)
    part = scatter_sum(part, z, COL, shift_z)
    part = part + lax.ppermute(part, ROW, SWAP_Z)
    part = part + lax.ppermute(part, ROW, SWAP_CORE)
    part = gather_back(part, z, COL, shift_z)
    part = gather_back(part, x, COL, shift_x)
    return gather_back(part, y, ROW, shift_y)


def node_part(features, cotangent, degree_wide, neighbour_sum, w_self, w_neigh):
    aggregate = (neighbour_sum / degree_wide).astype(BF16)
    preact = jnp.dot(features, w_self, preferred_element_type=F32) + jnp.dot(
        aggregate, w_neigh, preferred_element_type=F32
    )
    gate = jax.nn.sigmoid(preact)
    activations = (preact * gate).astype(BF16)
    slope = gate * (1.0 + preact * (1.0 - gate))
    dpreact = (cotangent.astype(F32) * slope).astype(BF16)
    dscaled = (
        jnp.einsum("ng,fg->nf", dpreact, w_neigh, preferred_element_type=F32) / degree_wide
    ).astype(BF16)
    return activations, aggregate, dpreact, dscaled


def per_device(
    features, w_self, w_neigh, cotangent, degree, tile_rows, tile_cols, tile_edges, tile_count
):
    nodes, width = features.shape
    row, col = lax.axis_index(ROW), lax.axis_index(COL)
    x, z, y = col & 3, col >> 2, row >> 2
    pos = jnp.stack([x, z, y, (row >> 1) & 1, row & 1]).astype(I32)
    room = tile_rows.shape[0] + BLOCK

    with jax.named_scope("gather_features"):
        across = lax.ppermute(features, ROW, SWAP_Z)
        near = [features, across]
        for k in (1, 2, 3):
            near += [lax.ppermute(p, ROW, shift_y(k)) for p in (features, across)]
        feature_pieces = near + [lax.ppermute(p, ROW, SWAP_CORE) for p in near]
    fslot, fsrc, fdst, bslot, bsrc, bdst, counts = make_lists(
        pos, tile_count, tile_rows, tile_cols, room
    )
    forward_masks = make_masks(True, fslot, tile_edges)
    backward_masks = make_masks(False, bslot, tile_edges)

    chunk_nodes = nodes // 2
    degree_wide = degree.astype(F32)[:, None]
    activations, aggregates, dpreacts, gathered = [], [], [], []
    for chunk in range(2):
        mine = slice(chunk * chunk_nodes, (chunk + 1) * chunk_nodes)
        pieces = products(chunk, 4, counts, fsrc, fdst, forward_masks, feature_pieces)
        with jax.named_scope("sum_along_x"):
            along_x = add_up(exchange(pieces, COL, shift_x))
        with jax.named_scope("sum_along_z"):
            rounded = along_x.astype(BF16)
            by_z = [along_x[:chunk_nodes]] + [
                rounded[k * chunk_nodes : (k + 1) * chunk_nodes] for k in (1, 2, 3)
            ]
            neighbour_sum = add_up(exchange(by_z, COL, shift_z))
        act, aggregate, dpreact, dscaled = node_part(
            features[mine], cotangent[mine], degree_wide[mine], neighbour_sum, w_self, w_neigh
        )
        activations.append(act)
        aggregates.append(aggregate)
        dpreacts.append(dpreact)
        with jax.named_scope("gather_dscaled"):
            own_x = spread(dscaled, COL, shift_x)
            from_z = spread(dscaled, COL, shift_z)
            rest_x = spread(jnp.concatenate(from_z), COL, shift_x)
            gathered += [dscaled] + from_z
            for own, rest in zip(own_x, rest_x):
                gathered += [own, rest]

    aggregate, dpreact = jnp.concatenate(aggregates), jnp.concatenate(dpreacts)
    with jax.named_scope("weight_grads"):
        grads = jnp.concatenate(
            [
                jnp.einsum("nf,ng->fg", features, dpreact, preferred_element_type=F32),
                jnp.einsum("nf,ng->fg", aggregate, dpreact, preferred_element_type=F32),
            ]
        )
        grads = sum_weights(grads, x, z, y)
    [for_other] = products(3, 1, counts, bsrc, bdst, backward_masks, gathered)
    from_other = lax.ppermute(for_other, ROW, SWAP_CORE)
    [own] = products(2, 1, counts, bsrc, bdst, backward_masks, gathered)
    with jax.named_scope("sum_along_y"):
        both = add_up([own, from_other])
        size = both.shape[0] // 4
        by_y = [both[:size]] + [both[k * size : (k + 1) * size].astype(BF16) for k in (1, 2, 3)]
        along_y = add_up(exchange(by_y, ROW, shift_y))
    with jax.named_scope("sum_across_z"):
        neighbour_grad = along_y[:nodes] + lax.ppermute(
            along_y[nodes:].astype(BF16), ROW, SWAP_Z
        ).astype(F32)
    own_grad = jnp.einsum("ng,fg->nf", dpreact, w_self, preferred_element_type=F32)
    feature_grad = (own_grad + neighbour_grad).astype(BF16)
    total_nodes = nodes * lax.axis_size(ROW) * lax.axis_size(COL)
    grads = grads * (1.0 / math.sqrt(total_nodes))
    return jnp.concatenate(activations), feature_grad, grads[:width], grads[width:]


def solution(mesh):
    by_device = P((ROW, COL))
    return jax.shard_map(
        per_device,
        mesh=mesh,
        in_specs=(
            P((ROW, COL), None),
            P(),
            P(),
            P((ROW, COL), None),
            by_device,
            by_device,
            by_device,
            P(None, (ROW, COL), None),
            by_device,
        ),
        out_specs=(P((ROW, COL), None), P((ROW, COL), None), P(), P()),
        check_vma=False,
    )
```

```python
import functools
import math

import jax
import jax.numpy as jnp
from jax import lax
from jax.experimental import pallas as pl
from jax.experimental.pallas import tpu as pltpu
from jax.sharding import PartitionSpec as P

F32, BF16, I32 = jnp.float32, jnp.bfloat16, jnp.int32
ROW, COL = "row", "col"
UNROLL = 8
BLOCK = 32
VMEM_LIMIT = 56 << 20


def shift_x(k):
    return [(4 * z + x, 4 * z + (x + k) % 4) for z in range(4) for x in range(4)]


def shift_z(k):
    return [(4 * z + x, 4 * ((z + k) % 4) + x) for z in range(4) for x in range(4)]


def shift_y(k):
    return [(4 * y + i, 4 * ((y + k) % 4) + i) for y in range(4) for i in range(4)]


SWAP_Z = [(i, i ^ 2) for i in range(16)]
SWAP_CORE = [(i, i ^ 1) for i in range(16)]


def list_kernel(pos, count, rows, cols, fslot, fsrc, fdst, bslot, bsrc, bdst, counts):
    room = fslot.shape[0]

    def clear(i, _):
        fslot[i] = 0
        fsrc[i] = 0
        fdst[i] = 32
        bslot[i] = 0
        bsrc[i] = 0
        bdst[i] = 32
        return 0

    lax.fori_loop(0, room, clear, 0)
    x, z, y, zl, core = pos[0], pos[1], pos[2], pos[3], pos[4]

    def place(s, held):
        f0, f1, b0, b1 = held
        row, col = rows[s], cols[s]
        tile, chunk = row & 1, (row >> 1) & 1
        rx, rz = (row >> 2) & 3, row >> 4
        ccore, czl, cy = (col >> 2) & 1, (col >> 3) & 1, col >> 4
        other = ccore ^ core
        half = (czl ^ zl) * 4 + (col & 3)
        fp = jnp.where(chunk == 0, f0, room - 1 - f1)
        fslot[fp] = s
        fsrc[fp] = other * 32 + ((y - cy) & 3) * 8 + half
        fdst[fp] = ((rx - x) & 3) * 8 + ((rz - z) & 3) * 2 + tile
        bp = jnp.where(other == 0, b0, room - 1 - b1)
        bslot[bp] = s
        bsrc[bp] = chunk * 32 + ((x - rx) & 3) * 8 + ((z - rz) & 3) * 2 + tile
        bdst[bp] = ((cy - y) & 3) * 8 + half
        return (f0 + 1 - chunk, f1 + chunk, b0 + 1 - other, b1 + other)

    zero = jnp.int32(0)
    held = lax.fori_loop(0, count[0], place, (zero, zero, zero, zero))
    for i in range(4):
        counts[i] = held[i]


def make_lists(pos, count, rows, cols, room):
    smem = pl.BlockSpec(memory_space=pltpu.SMEM)
    return pl.pallas_call(
        list_kernel,
        out_shape=[jax.ShapeDtypeStruct((room,), I32)] * 6 + [jax.ShapeDtypeStruct((8,), I32)],
        in_specs=[smem] * 4,
        out_specs=[smem] * 7,
        name="slot_lists",
    )(pos, count, rows, cols)


def mask_kernel(flip, slots, edges, out):
    base = pl.program_id(0) * BLOCK
    tile = out.shape[1]
    column = lax.broadcasted_iota(I32, (tile, tile), 0)
    edge_count = edges.shape[0]

    def one(i, _):
        s = slots[base + i]
        total = jnp.zeros((tile, tile), F32)
        for k in range(edge_count):
            total += jnp.where(edges[k, pl.ds(s, 1), :] == column, 1.0, 0.0)
        out[i] = (total.T if flip else total).astype(BF16)
        return 0

    lax.fori_loop(0, BLOCK, one, 0, unroll=4)


def make_masks(flip, slots, edges):
    room, tile = slots.shape[0], edges.shape[2]
    return pl.pallas_call(
        functools.partial(mask_kernel, flip),
        grid=(room // BLOCK,),
        out_shape=jax.ShapeDtypeStruct((room, tile, tile), BF16),
        in_specs=[
            pl.BlockSpec(memory_space=pltpu.SMEM),
            pl.BlockSpec(edges.shape, lambda i: (0, 0, 0)),
        ],
        out_specs=pl.BlockSpec((BLOCK, tile, tile), lambda i: (i, 0, 0)),
        cost_estimate=pl.CostEstimate(
            flops=room * tile * tile * 12, bytes_accessed=room * tile * tile * 2, transcendentals=0
        ),
        name="one_hot_tiles",
    )(slots, edges)


def product_kernel(side, n_in, n_out, counts, src, dst, masks, *refs):
    ins, outs = refs[:n_in], refs[n_in : n_in + n_out]
    held, tiles, total, staged, in_sems, tile_sems, out_sems = refs[n_in + n_out :]
    room, tile = masks.shape[0], masks.shape[1]
    n = counts[side]
    copies, at = [], 0
    for i, ref in enumerate(ins):
        size = ref.shape[0]
        copies.append(pltpu.make_async_copy(ref, held.at[pl.ds(at, size)], in_sems.at[i]))
        at += size
    blocks = (room - BLOCK) // BLOCK

    def block_copy(k):
        first = (k if side % 2 == 0 else room // BLOCK - 1 - k) * BLOCK
        part = pl.ds(first, BLOCK)
        return pltpu.make_async_copy(masks.at[part], tiles.at[part], tile_sems.at[k])

    for copy in copies:
        copy.start()
    for k in range(blocks):
        pl.when(n > k * BLOCK)(lambda k=k: block_copy(k).start())
    n_total = total.shape[0] - 1

    def clear(i, _):
        total[i] = jnp.zeros(total.shape[1:], F32)
        return 0

    lax.fori_loop(0, n_total, clear, 0)
    for copy in copies:
        copy.wait()
    for k in range(blocks):
        pl.when(n > k * BLOCK)(lambda k=k: block_copy(k).wait())
    steps = (n + UNROLL - 1) // UNROLL
    low = 0 if side % 2 == 0 else room - steps * UNROLL

    def step(i, _):
        first = low + i * UNROLL
        for half in range(0, UNROLL, 4):
            parts = [
                jnp.dot(
                    tiles[first + u],
                    held[pl.ds(pl.multiple_of(src[first + u] * tile, tile), tile), :],
                    preferred_element_type=F32,
                )
                for u in range(half, half + 4)
            ]
            for u in range(4):
                total[dst[first + half + u]] += parts[u]
        return 0

    lax.fori_loop(0, steps, step, 0)
    per = n_total // n_out
    sends = []
    for o, ref in enumerate(outs):

        def convert(i, _, o=o):
            j = o * per + i
            staged[pl.ds(pl.multiple_of(j * tile, tile), tile), :] = total[j].astype(BF16)
            return 0

        lax.fori_loop(0, per, convert, 0)
        rows = per * tile
        sends.append(pltpu.make_async_copy(staged.at[pl.ds(o * rows, rows)], ref, out_sems.at[o]))
        sends[-1].start()
    for send in sends:
        send.wait()


def products(side, n_out, counts, src, dst, masks, pieces):
    tile, width = masks.shape[1], pieces[0].shape[1]
    n_in, rows = len(pieces), sum(p.shape[0] for p in pieces)
    smem, anywhere = pl.BlockSpec(memory_space=pltpu.SMEM), pl.BlockSpec(memory_space=pl.ANY)
    return pl.pallas_call(
        functools.partial(product_kernel, side, n_in, n_out),
        out_shape=[jax.ShapeDtypeStruct((32 * tile // n_out, width), BF16)] * n_out,
        in_specs=[smem] * 3 + [anywhere] * (1 + n_in),
        out_specs=[anywhere] * n_out,
        scratch_shapes=[
            pltpu.VMEM((rows, width), BF16),
            pltpu.VMEM(masks.shape, BF16),
            pltpu.VMEM((33, tile, width), F32),
            pltpu.VMEM((32 * tile, width), BF16),
            pltpu.SemaphoreType.DMA((n_in,)),
            pltpu.SemaphoreType.DMA((masks.shape[0] // BLOCK,)),
            pltpu.SemaphoreType.DMA((n_out,)),
        ],
        compiler_params=pltpu.CompilerParams(vmem_limit_bytes=VMEM_LIMIT),
        cost_estimate=pl.CostEstimate(
            flops=128 * tile * tile * width * 2 * 4, bytes_accessed=12 << 20, transcendentals=0
        ),
        name="tile_products",
    )(counts, src, dst, masks, *pieces)


def spread(value, axis, shift):
    return [lax.ppermute(value, axis, shift(k)) for k in (1, 2, 3)]


def exchange(pieces, axis, shift):
    return [pieces[0]] + [lax.ppermute(pieces[k], axis, shift(k)) for k in (1, 2, 3)]


def add_up(parts):
    total = parts[0].astype(F32)
    for part in parts[1:]:
        total = total + part.astype(F32)
    return total


def scatter_sum(value, index, axis, shift):
    size = value.shape[0] // 4
    pieces = [lax.dynamic_slice_in_dim(value, ((index + k) & 3) * size, size) for k in range(4)]
    return add_up(exchange(pieces, axis, shift))


def gather_back(value, index, axis, shift):
    size = value.shape[0]
    full = jnp.zeros((4 * size, value.shape[1]), value.dtype)
    for k, piece in enumerate([value] + spread(value, axis, shift)):
        full = lax.dynamic_update_slice_in_dim(full, piece, ((index - k) & 3) * size, 0)
    return full


def sum_all(value, axis, shift):
    return add_up([value] + spread(value, axis, shift))


def node_part(features, cotangent, degree_wide, neighbour_sum, w_self, w_neigh):
    aggregate = (neighbour_sum / degree_wide).astype(BF16)
    preact = jnp.dot(features, w_self, preferred_element_type=F32) + jnp.dot(
        aggregate, w_neigh, preferred_element_type=F32
    )
    gate = jax.nn.sigmoid(preact)
    activations = (preact * gate).astype(BF16)
    slope = gate * (1.0 + preact * (1.0 - gate))
    dpreact = (cotangent.astype(F32) * slope).astype(BF16)
    dscaled = (
        jnp.einsum("ng,fg->nf", dpreact, w_neigh, preferred_element_type=F32) / degree_wide
    ).astype(BF16)
    return activations, aggregate, dpreact, dscaled


def per_device(
    features, w_self, w_neigh, cotangent, degree, tile_rows, tile_cols, tile_edges, tile_count
):
    nodes, width = features.shape
    row, col = lax.axis_index(ROW), lax.axis_index(COL)
    x, z, y = col & 3, col >> 2, row >> 2
    pos = jnp.stack([x, z, y, (row >> 1) & 1, row & 1]).astype(I32)
    room = tile_rows.shape[0] + BLOCK

    with jax.named_scope("gather_features"):
        across = lax.ppermute(features, ROW, SWAP_Z)
        near = [features, across]
        for k in (1, 2, 3):
            near += [lax.ppermute(p, ROW, shift_y(k)) for p in (features, across)]
    fslot, fsrc, fdst, bslot, bsrc, bdst, counts = make_lists(
        pos, tile_count, tile_rows, tile_cols, room
    )
    forward_masks = make_masks(True, fslot, tile_edges)
    forward_masks, *near = lax.optimization_barrier((forward_masks, *near))
    with jax.named_scope("gather_features"):
        feature_pieces = near + [lax.ppermute(p, ROW, SWAP_CORE) for p in near]

    chunk_nodes = nodes // 2
    degree_wide = degree.astype(F32)[:, None]
    activations, aggregates, dpreacts, gathered = [], [], [], []
    for chunk in range(2):
        mine = slice(chunk * chunk_nodes, (chunk + 1) * chunk_nodes)
        pieces = products(chunk, 4, counts, fsrc, fdst, forward_masks, feature_pieces)
        with jax.named_scope("sum_along_x"):
            along_x = add_up(exchange(pieces, COL, shift_x))
        with jax.named_scope("sum_along_z"):
            rounded = along_x.astype(BF16)
            by_z = [along_x[:chunk_nodes]] + [
                rounded[k * chunk_nodes : (k + 1) * chunk_nodes] for k in (1, 2, 3)
            ]
            neighbour_sum = add_up(exchange(by_z, COL, shift_z))
        act, aggregate, dpreact, dscaled = node_part(
            features[mine], cotangent[mine], degree_wide[mine], neighbour_sum, w_self, w_neigh
        )
        activations.append(act)
        aggregates.append(aggregate)
        dpreacts.append(dpreact)
        with jax.named_scope("gather_dscaled"):
            own_x = spread(dscaled, COL, shift_x)
            from_z = spread(dscaled, COL, shift_z)
            rest_x = spread(jnp.concatenate(from_z), COL, shift_x)
            gathered += [dscaled] + from_z
            for own, rest in zip(own_x, rest_x):
                gathered += [own, rest]

    aggregate, dpreact = jnp.concatenate(aggregates), jnp.concatenate(dpreacts)
    with jax.named_scope("weight_grads"):
        grads = jnp.concatenate(
            [
                jnp.einsum("nf,ng->fg", features, dpreact, preferred_element_type=F32),
                jnp.einsum("nf,ng->fg", aggregate, dpreact, preferred_element_type=F32),
            ]
        )
        grads = scatter_sum(grads, y, ROW, shift_y)
    grads, *gathered = lax.optimization_barrier((grads, *gathered))
    with jax.named_scope("weight_grads"):
        grads = sum_all(grads, COL, shift_x)
    backward_masks = make_masks(False, bslot, tile_edges)
    [for_other] = products(3, 1, counts, bsrc, bdst, backward_masks, gathered)
    grads, for_other = lax.optimization_barrier((grads, for_other))
    from_other = lax.ppermute(for_other, ROW, SWAP_CORE)
    with jax.named_scope("weight_grads"):
        grads = sum_all(grads, COL, shift_z)
    [own] = products(2, 1, counts, bsrc, bdst, backward_masks, gathered)
    with jax.named_scope("sum_along_y"):
        both = add_up([own, from_other])
        size = both.shape[0] // 4
        by_y = [both[:size]] + [both[k * size : (k + 1) * size].astype(BF16) for k in (1, 2, 3)]
    grads, *by_y = lax.optimization_barrier((grads, *by_y))
    with jax.named_scope("sum_along_y"):
        along_y = add_up(exchange(by_y, ROW, shift_y))
    with jax.named_scope("weight_grads"):
        grads = grads + lax.ppermute(grads, ROW, SWAP_Z)
        grads = grads + lax.ppermute(grads, ROW, SWAP_CORE)
    grads, along_y = lax.optimization_barrier((grads, along_y))
    with jax.named_scope("sum_across_z"):
        neighbour_grad = along_y[:nodes] + lax.ppermute(
            along_y[nodes:].astype(BF16), ROW, SWAP_Z
        ).astype(F32)
    with jax.named_scope("weight_grads"):
        grads = gather_back(grads, y, ROW, shift_y)
    own_grad = jnp.einsum("ng,fg->nf", dpreact, w_self, preferred_element_type=F32)
    feature_grad = (own_grad + neighbour_grad).astype(BF16)
    total_nodes = nodes * lax.axis_size(ROW) * lax.axis_size(COL)
    grads = grads * (1.0 / math.sqrt(total_nodes))
    return jnp.concatenate(activations), feature_grad, grads[:width], grads[width:]


def solution(mesh):
    by_device = P((ROW, COL))
    return jax.shard_map(
        per_device,
        mesh=mesh,
        in_specs=(
            P((ROW, COL), None),
            P(),
            P(),
            P((ROW, COL), None),
            by_device,
            by_device,
            by_device,
            P(None, (ROW, COL), None),
            by_device,
        ),
        out_specs=(P((ROW, COL), None), P((ROW, COL), None), P(), P()),
        check_vma=False,
    )
```

```python
import functools
import math

import jax
import jax.numpy as jnp
from jax import lax
from jax.experimental import pallas as pl
from jax.experimental.pallas import tpu as pltpu
from jax.sharding import PartitionSpec as P

F32, BF16, I32 = jnp.float32, jnp.bfloat16, jnp.int32
ROW, COL = "row", "col"
UNROLL = 8
BLOCK = 32
VMEM_LIMIT = 56 << 20


def shift_x(k):
    return [(4 * z + x, 4 * z + (x + k) % 4) for z in range(4) for x in range(4)]


def shift_z(k):
    return [(4 * z + x, 4 * ((z + k) % 4) + x) for z in range(4) for x in range(4)]


def shift_y(k):
    return [(4 * y + i, 4 * ((y + k) % 4) + i) for y in range(4) for i in range(4)]


SWAP_Z = [(i, i ^ 2) for i in range(16)]
SWAP_CORE = [(i, i ^ 1) for i in range(16)]


LISTS = 6


def list_kernel(pos, count, rows, cols, slot, src, dst, counts):
    stretch = slot.shape[0] // LISTS
    x, z, y, zl, core = pos[0], pos[1], pos[2], pos[3], pos[4]
    for i in range(LISTS):
        counts[i] = 0

    def place(s, _):
        row, col = rows[s], cols[s]
        tile, chunk = row & 1, (row >> 1) & 1
        rx, rz = (row >> 2) & 3, row >> 4
        ccore, czl, cy = (col >> 2) & 1, (col >> 3) & 1, col >> 4
        other = ccore ^ core
        half = (czl ^ zl) * 4 + (col & 3)
        n = counts[chunk]
        counts[chunk] = n + 1
        at = chunk * stretch + n
        slot[at] = s
        src[at] = other * 32 + ((y - cy) & 3) * 8 + half
        dst[at] = ((rx - x) & 3) * 8 + ((rz - z) & 3) * 2 + tile
        which = 2 + 2 * chunk + other
        n = counts[which]
        counts[which] = n + 1
        at = which * stretch + n
        slot[at] = s
        src[at] = ((x - rx) & 3) * 8 + ((z - rz) & 3) * 2 + tile
        dst[at] = ((cy - y) & 3) * 8 + half
        return 0

    lax.fori_loop(0, count[0], place, 0)
    for i in range(LISTS):
        end = i * stretch + counts[i]
        for u in range(UNROLL):
            slot[end + u] = 0
            src[end + u] = 0
            dst[end + u] = 32


def make_lists(pos, count, rows, cols):
    smem = pl.BlockSpec(memory_space=pltpu.SMEM)
    length = LISTS * (rows.shape[0] + UNROLL)
    return pl.pallas_call(
        list_kernel,
        out_shape=[jax.ShapeDtypeStruct((length,), I32)] * 3 + [jax.ShapeDtypeStruct((8,), I32)],
        in_specs=[smem] * 4,
        out_specs=[smem] * 4,
        name="slot_lists",
    )(pos, count, rows, cols)


def mask_kernel(which, flip, counts, slots, edges, out):
    block = pl.program_id(0) * BLOCK
    base = which * (slots.shape[0] // LISTS) + block
    tile = out.shape[1]
    column = lax.broadcasted_iota(I32, (tile, tile), 0)
    edge_count = edges.shape[0]
    used = (counts[which] + UNROLL - 1) // UNROLL * UNROLL

    @pl.loop(0, jnp.clip(used - block, 0, BLOCK) // UNROLL)
    def _(group):
        for u in range(UNROLL):
            i = group * UNROLL + u
            s = slots[base + i]
            total = jnp.zeros((tile, tile), F32)
            for k in range(edge_count):
                total += jnp.where(edges[k, pl.ds(s, 1), :] == column, 1.0, 0.0)
            out[i] = (total.T if flip else total).astype(BF16)


def make_masks(which, flip, counts, slots, edges):
    room, tile = edges.shape[1], edges.shape[2]
    smem = pl.BlockSpec(memory_space=pltpu.SMEM)
    return pl.pallas_call(
        functools.partial(mask_kernel, which, flip),
        grid=(room // BLOCK,),
        out_shape=jax.ShapeDtypeStruct((room, tile, tile), BF16),
        in_specs=[smem, smem, pl.BlockSpec(edges.shape, lambda i: (0, 0, 0))],
        out_specs=pl.BlockSpec((BLOCK, tile, tile), lambda i: (i, 0, 0)),
        cost_estimate=pl.CostEstimate(
            flops=room * tile * tile * 12, bytes_accessed=room * tile * tile * 2, transcendentals=0
        ),
        name="one_hot_tiles",
    )(counts, slots, edges)


def product_kernel(which, n_in, n_out, carried, raw, counts, src, dst, masks, *refs):
    ins, refs = refs[:n_in], refs[n_in:]
    first, refs = (refs[0], refs[1:]) if carried else (None, refs)
    outs, refs = refs[:n_out], refs[n_out:]
    held, tiles, total, staged, in_sems, tile_sems, out_sems = refs
    room, tile, width = masks.shape[0], masks.shape[1], held.shape[1]
    n = counts[which]
    base = which * (src.shape[0] // LISTS)
    copies, at = [], 0
    for i, ref in enumerate(ins):
        size = ref.shape[0]
        copies.append(pltpu.make_async_copy(ref, held.at[pl.ds(at, size)], in_sems.at[i]))
        at += size
    results = total.shape[0] - tile
    if carried:
        copies.append(pltpu.make_async_copy(first, total.at[pl.ds(0, results)], in_sems.at[n_in]))

    def block_copy(k):
        part = pl.ds(k * BLOCK, BLOCK)
        return pltpu.make_async_copy(masks.at[part], tiles.at[part], tile_sems.at[k])

    for copy in copies:
        copy.start()
    for k in range(room // BLOCK):
        pl.when(n > k * BLOCK)(lambda k=k: block_copy(k).start())
    if not carried:

        @pl.loop(0, results // tile)
        def _(i):
            total[pl.ds(pl.multiple_of(i * tile, tile), tile), :] = jnp.zeros((tile, width), F32)

    for copy in copies:
        copy.wait()
    for k in range(room // BLOCK):
        pl.when(n > k * BLOCK)(lambda k=k: block_copy(k).wait())

    @pl.loop(0, (n + UNROLL - 1) // UNROLL)
    def _(i):
        for half in range(0, UNROLL, 4):
            at = [i * UNROLL + half + u for u in range(4)]
            parts = [
                jnp.dot(
                    tiles[p],
                    held[pl.ds(pl.multiple_of(src[base + p] * tile, tile), tile), :],
                    preferred_element_type=F32,
                )
                for p in at
            ]
            for p, part in zip(at, parts):
                total[pl.ds(pl.multiple_of(dst[base + p] * tile, tile), tile), :] += part

    rows = results // n_out
    sends = []
    for o, ref in enumerate(outs):
        if raw:
            source = total.at[pl.ds(o * rows, rows)]
        else:
            source = staged.at[pl.ds(o * rows, rows)]

            @pl.loop(0, rows // tile)
            def _(i, o=o):
                part = pl.ds(pl.multiple_of(o * rows + i * tile, tile), tile)
                staged[part, :] = total[part, :].astype(BF16)

        sends.append(pltpu.make_async_copy(source, ref, out_sems.at[o]))
        sends[-1].start()
    for send in sends:
        send.wait()


def products(which, n_out, lists, masks, pieces, first=None, raw=False):
    slot, src, dst, counts = lists
    tile, width = masks.shape[1], pieces[0].shape[1]
    n_in, rows = len(pieces), sum(p.shape[0] for p in pieces)
    carried = first is not None
    smem, anywhere = pl.BlockSpec(memory_space=pltpu.SMEM), pl.BlockSpec(memory_space=pl.ANY)
    return pl.pallas_call(
        functools.partial(product_kernel, which, n_in, n_out, carried, raw),
        out_shape=[jax.ShapeDtypeStruct((32 * tile // n_out, width), F32 if raw else BF16)] * n_out,
        in_specs=[smem] * 3 + [anywhere] * (1 + n_in + carried),
        out_specs=[anywhere] * n_out,
        scratch_shapes=[
            pltpu.VMEM((rows, width), BF16),
            pltpu.VMEM(masks.shape, BF16),
            pltpu.VMEM((33 * tile, width), F32),
            pltpu.VMEM((8, 128) if raw else (32 * tile, width), BF16),
            pltpu.SemaphoreType.DMA((n_in + 1,)),
            pltpu.SemaphoreType.DMA((masks.shape[0] // BLOCK,)),
            pltpu.SemaphoreType.DMA((n_out,)),
        ],
        compiler_params=pltpu.CompilerParams(vmem_limit_bytes=VMEM_LIMIT),
        cost_estimate=pl.CostEstimate(
            flops=128 * tile * tile * width * 2 * 4, bytes_accessed=12 << 20, transcendentals=0
        ),
        name="tile_products",
    )(counts, src, dst, masks, *pieces, *([first] if carried else []))


def spread(value, axis, shift):
    return [lax.ppermute(value, axis, shift(k)) for k in (1, 2, 3)]


def exchange(pieces, axis, shift):
    return [pieces[0]] + [lax.ppermute(pieces[k], axis, shift(k)) for k in (1, 2, 3)]


def add_up(parts):
    total = parts[0].astype(F32)
    for part in parts[1:]:
        total = total + part.astype(F32)
    return total


def scatter_sum(value, index, axis, shift):
    size = value.shape[0] // 4
    pieces = [lax.dynamic_slice_in_dim(value, ((index + k) & 3) * size, size) for k in range(4)]
    return add_up(exchange(pieces, axis, shift))


def gather_back(value, index, axis, shift):
    size = value.shape[0]
    full = jnp.zeros((4 * size, value.shape[1]), value.dtype)
    for k, piece in enumerate([value] + spread(value, axis, shift)):
        full = lax.dynamic_update_slice_in_dim(full, piece, ((index - k) & 3) * size, 0)
    return full


def sum_all(value, axis, shift):
    return add_up([value] + spread(value, axis, shift))


def node_part(features, cotangent, degree_wide, neighbour_sum, w_self, w_neigh):
    aggregate = (neighbour_sum / degree_wide).astype(BF16)
    preact = jnp.dot(features, w_self, preferred_element_type=F32) + jnp.dot(
        aggregate, w_neigh, preferred_element_type=F32
    )
    gate = jax.nn.sigmoid(preact)
    activations = (preact * gate).astype(BF16)
    slope = gate * (1.0 + preact * (1.0 - gate))
    dpreact = (cotangent.astype(F32) * slope).astype(BF16)
    dscaled = (
        jnp.einsum("ng,fg->nf", dpreact, w_neigh, preferred_element_type=F32) / degree_wide
    ).astype(BF16)
    return activations, aggregate, dpreact, dscaled


def per_device(
    features, w_self, w_neigh, cotangent, degree, tile_rows, tile_cols, tile_edges, tile_count
):
    nodes, width = features.shape
    row, col = lax.axis_index(ROW), lax.axis_index(COL)
    x, z, y = col & 3, col >> 2, row >> 2
    pos = jnp.stack([x, z, y, (row >> 1) & 1, row & 1]).astype(I32)

    with jax.named_scope("gather_features"):
        across = lax.ppermute(features, ROW, SWAP_Z)
        near = [features, across]
        for k in (1, 2, 3):
            near += [lax.ppermute(p, ROW, shift_y(k)) for p in (features, across)]
    lists = make_lists(pos, tile_count, tile_rows, tile_cols)
    slot, counts = lists[0], lists[3]
    counts, *near = lax.optimization_barrier((counts, *near))
    with jax.named_scope("gather_features"):
        feature_pieces = near + [lax.ppermute(p, ROW, SWAP_CORE) for p in near]

    degree_wide = degree.astype(F32)[:, None]
    parts = [slice(0, nodes // 2), slice(nodes // 2, nodes)]

    def sum_along_x(pieces):
        with jax.named_scope("sum_along_x"):
            along_x = add_up(exchange(pieces, COL, shift_x))
            rounded = along_x.astype(BF16)
            size = along_x.shape[0] // 4
            return [along_x[:size]] + [rounded[k * size : (k + 1) * size] for k in (1, 2, 3)]

    def finish_nodes(by_z, mine):
        with jax.named_scope("sum_along_z"):
            neighbour_sum = add_up(exchange(by_z, COL, shift_z))
        return node_part(
            features[mine], cotangent[mine], degree_wide[mine], neighbour_sum, w_self, w_neigh
        )

    def gather_z(dscaled):
        with jax.named_scope("gather_dscaled"):
            return [dscaled] + spread(dscaled, COL, shift_z)

    def gather_x(from_z):
        with jax.named_scope("gather_dscaled"):
            line = jnp.concatenate(from_z)
            return [line] + spread(line, COL, shift_x)

    tie = lax.optimization_barrier
    masks = make_masks(0, True, counts, slot, tile_edges)
    pieces_a = products(0, 4, lists, masks, feature_pieces)
    masks = make_masks(1, True, counts, slot, tile_edges)
    pieces_b = products(1, 4, lists, masks, feature_pieces)
    counts, pieces_b = tie((counts, pieces_b))
    masks_a = [make_masks(2 + side, False, counts, slot, tile_edges) for side in (1, 0)]
    by_z_a, masks_a, counts = tie((sum_along_x(pieces_a), masks_a, counts))
    masks_b = [make_masks(4 + side, False, counts, slot, tile_edges) for side in (1, 0)]
    by_z_b, masks_b = tie((sum_along_x(pieces_b), masks_b))
    act_a, aggregate_a, dpreact_a, dscaled_a = finish_nodes(by_z_a, parts[0])
    from_z_a, by_z_b = tie((gather_z(dscaled_a), by_z_b))
    gathered_a = gather_x(from_z_a)
    act_b, aggregate_b, dpreact_b, dscaled_b = finish_nodes(by_z_b, parts[1])
    from_z_b = gather_z(dscaled_b)
    gathered_b = gather_x(from_z_b)

    aggregate = jnp.concatenate([aggregate_a, aggregate_b])
    dpreact = jnp.concatenate([dpreact_a, dpreact_b])
    with jax.named_scope("weight_grads"):
        grads = jnp.concatenate(
            [
                jnp.einsum("nf,ng->fg", features, dpreact, preferred_element_type=F32),
                jnp.einsum("nf,ng->fg", aggregate, dpreact, preferred_element_type=F32),
            ]
        )
    grads, from_z_b = tie((grads, from_z_b))
    with jax.named_scope("weight_grads"):
        grads = scatter_sum(grads, y, ROW, shift_y)
        grads = grads + lax.ppermute(grads, ROW, SWAP_Z)
        grads = grads + lax.ppermute(grads, ROW, SWAP_CORE)
    sums_a = [
        products(2 + side, 1, lists, masks_a[1 - side], gathered_a, raw=True)[0] for side in (1, 0)
    ]
    sums_a, grads, gathered_b = tie((sums_a, grads, gathered_b))
    with jax.named_scope("weight_grads"):
        grads = sum_all(grads, COL, shift_x)
    [for_other] = products(5, 1, lists, masks_b[0], gathered_b, first=sums_a[0])
    grads, for_other = tie((grads, for_other))
    from_other = lax.ppermute(for_other, ROW, SWAP_CORE)
    with jax.named_scope("weight_grads"):
        grads = sum_all(grads, COL, shift_z)
    [own] = products(4, 1, lists, masks_b[1], gathered_b, first=sums_a[1])
    with jax.named_scope("sum_along_y"):
        both = add_up([own, from_other])
        size = both.shape[0] // 4
        by_y = [both[:size]] + [both[k * size : (k + 1) * size].astype(BF16) for k in (1, 2, 3)]
    with jax.named_scope("sum_along_y"):
        received = exchange(by_y, ROW, shift_y)
        along_y = add_up(received)
        for_across, along_y = along_y[nodes:].astype(BF16), along_y[:nodes]
    with jax.named_scope("sum_across_z"):
        neighbour_grad = along_y + lax.ppermute(for_across, ROW, SWAP_Z).astype(F32)
    with jax.named_scope("weight_grads"):
        grads = gather_back(grads, y, ROW, shift_y)
    own_grad = jnp.einsum("ng,fg->nf", dpreact, w_self, preferred_element_type=F32)
    feature_grad = (own_grad + neighbour_grad).astype(BF16)
    total_nodes = nodes * lax.axis_size(ROW) * lax.axis_size(COL)
    grads = grads * (1.0 / math.sqrt(total_nodes))
    return jnp.concatenate([act_a, act_b]), feature_grad, grads[:width], grads[width:]


def solution(mesh):
    by_device = P((ROW, COL))
    return jax.shard_map(
        per_device,
        mesh=mesh,
        in_specs=(
            P((ROW, COL), None),
            P(),
            P(),
            P((ROW, COL), None),
            by_device,
            by_device,
            by_device,
            P(None, (ROW, COL), None),
            by_device,
        ),
        out_specs=(P((ROW, COL), None), P((ROW, COL), None), P(), P()),
        check_vma=False,
    )
```

```python
import functools
import math

import jax
import jax.numpy as jnp
from jax import lax
from jax.experimental import pallas as pl
from jax.experimental.pallas import tpu as pltpu
from jax.sharding import PartitionSpec as P

F32, BF16, I32 = jnp.float32, jnp.bfloat16, jnp.int32
ROW, COL = "row", "col"
UNROLL = 8
VMEM_LIMIT = 32 << 20


def shift_x(k):
    return [(4 * z + x, 4 * z + (x + k) % 4) for z in range(4) for x in range(4)]


def shift_z(k):
    return [(4 * z + x, 4 * ((z + k) % 4) + x) for z in range(4) for x in range(4)]


def shift_y(k):
    return [(4 * y + i, 4 * ((y + k) % 4) + i) for y in range(4) for i in range(4)]


SWAP_Z = [(i, i ^ 2) for i in range(16)]
SWAP_CORE = [(i, i ^ 1) for i in range(16)]


LISTS = 6


def list_kernel(pos, count, rows, cols, slot, src, dst, counts):
    stretch = slot.shape[0] // LISTS
    x, z, y, zl, core = pos[0], pos[1], pos[2], pos[3], pos[4]
    for i in range(LISTS):
        counts[i] = 0

    def place(s, _):
        row, col = rows[s], cols[s]
        tile, chunk = row & 1, (row >> 1) & 1
        rx, rz = (row >> 2) & 3, row >> 4
        ccore, czl, cy = (col >> 2) & 1, (col >> 3) & 1, col >> 4
        other = ccore ^ core
        half = (czl ^ zl) * 4 + (col & 3)
        n = counts[chunk]
        counts[chunk] = n + 1
        at = chunk * stretch + n
        slot[at] = s
        src[at] = other * 32 + ((y - cy) & 3) * 8 + half
        dst[at] = ((rx - x) & 3) * 8 + ((rz - z) & 3) * 2 + tile
        which = 2 + 2 * chunk + other
        n = counts[which]
        counts[which] = n + 1
        at = which * stretch + n
        slot[at] = s
        src[at] = ((x - rx) & 3) * 8 + ((z - rz) & 3) * 2 + tile
        dst[at] = ((cy - y) & 3) * 8 + half
        return 0

    lax.fori_loop(0, count[0], place, 0)
    for i in range(LISTS):
        end = i * stretch + counts[i]
        for u in range(UNROLL):
            slot[end + u] = 0
            src[end + u] = 0
            dst[end + u] = 32


def make_lists(pos, count, rows, cols):
    smem = pl.BlockSpec(memory_space=pltpu.SMEM)
    length = LISTS * (rows.shape[0] + UNROLL)
    return pl.pallas_call(
        list_kernel,
        out_shape=[jax.ShapeDtypeStruct((length,), I32)] * 3 + [jax.ShapeDtypeStruct((8,), I32)],
        in_specs=[smem] * 4,
        out_specs=[smem] * 4,
        name="slot_lists",
    )(pos, count, rows, cols)


def edge_tile(edges, s):
    edge_count, _, tile = edges.shape
    column = lax.broadcasted_iota(I32, (tile, tile), 0).astype(F32).astype(BF16)
    one, zero = jnp.ones((tile, tile), BF16), jnp.zeros((tile, tile), BF16)
    total = None
    for k in range(edge_count):
        edge = jnp.broadcast_to(edges[k, pl.ds(s, 1), :], (16, tile)).astype(F32).astype(BF16)
        match = jnp.where(jnp.concatenate([edge] * (tile // 16), axis=0) == column, one, zero)
        total = match if total is None else total + match
    return total


def product_kernel(which, n_in, n_out, carried, raw, counts, slot, src, dst, edges, *refs):
    ins, refs = refs[:n_in], refs[n_in:]
    first, refs = (refs[0], refs[1:]) if carried else (None, refs)
    outs, refs = refs[:n_out], refs[n_out:]
    held, total, staged, in_sems, out_sems = refs
    tile, width = edges.shape[2], held.shape[1]
    n = counts[which]
    base = which * (src.shape[0] // LISTS)
    copies, at = [], 0
    for i, ref in enumerate(ins):
        size = ref.shape[0]
        copies.append(pltpu.make_async_copy(ref, held.at[pl.ds(at, size)], in_sems.at[i]))
        at += size
    results = total.shape[0] - tile
    if carried:
        copies.append(pltpu.make_async_copy(first, total.at[pl.ds(0, results)], in_sems.at[n_in]))
    for copy in copies:
        copy.start()
    if not carried:

        @pl.loop(0, results // tile)
        def _(i):
            total[pl.ds(pl.multiple_of(i * tile, tile), tile), :] = jnp.zeros((tile, width), F32)

    for copy in copies:
        copy.wait()
    over = ((0,), (0,)) if which < 2 else ((1,), (0,))

    @pl.loop(0, (n + UNROLL - 1) // UNROLL)
    def _(i):
        for half in range(0, UNROLL, 4):
            at = [base + i * UNROLL + half + u for u in range(4)]
            parts = [
                lax.dot_general(
                    edge_tile(edges, slot[p]),
                    held[pl.ds(pl.multiple_of(src[p] * tile, tile), tile), :],
                    (over, ((), ())),
                    preferred_element_type=F32,
                )
                for p in at
            ]
            for p, part in zip(at, parts):
                total[pl.ds(pl.multiple_of(dst[p] * tile, tile), tile), :] += part

    rows = results // n_out
    sends = []
    for o, ref in enumerate(outs):
        if raw:
            source = total.at[pl.ds(o * rows, rows)]
        else:
            source = staged.at[pl.ds(o * rows, rows)]

            @pl.loop(0, rows // tile)
            def _(i, o=o):
                part = pl.ds(pl.multiple_of(o * rows + i * tile, tile), tile)
                staged[part, :] = total[part, :].astype(BF16)

        sends.append(pltpu.make_async_copy(source, ref, out_sems.at[o]))
        sends[-1].start()
    for send in sends:
        send.wait()


def products(which, n_out, lists, edges, pieces, first=None, raw=False):
    slot, src, dst, counts = lists
    tile, width = edges.shape[2], pieces[0].shape[1]
    n_in, rows = len(pieces), sum(p.shape[0] for p in pieces)
    carried = first is not None
    smem, anywhere = pl.BlockSpec(memory_space=pltpu.SMEM), pl.BlockSpec(memory_space=pl.ANY)
    return pl.pallas_call(
        functools.partial(product_kernel, which, n_in, n_out, carried, raw),
        out_shape=[jax.ShapeDtypeStruct((32 * tile // n_out, width), F32 if raw else BF16)] * n_out,
        in_specs=[smem] * 4 + [pl.BlockSpec(memory_space=pltpu.VMEM)] + [anywhere] * (n_in + carried),
        out_specs=[anywhere] * n_out,
        scratch_shapes=[
            pltpu.VMEM((rows, width), BF16),
            pltpu.VMEM((33 * tile, width), F32),
            pltpu.VMEM((16, 128) if raw else (32 * tile, width), BF16),
            pltpu.SemaphoreType.DMA((n_in + 1,)),
            pltpu.SemaphoreType.DMA((n_out,)),
        ],
        compiler_params=pltpu.CompilerParams(vmem_limit_bytes=VMEM_LIMIT),
        cost_estimate=pl.CostEstimate(
            flops=128 * tile * tile * width * 2 * 4, bytes_accessed=12 << 20, transcendentals=0
        ),
        name="tile_products",
    )(counts, slot, src, dst, edges, *pieces, *([first] if carried else []))


def spread(value, axis, shift):
    return [lax.ppermute(value, axis, shift(k)) for k in (1, 2, 3)]


def exchange(pieces, axis, shift):
    return [pieces[0]] + [lax.ppermute(pieces[k], axis, shift(k)) for k in (1, 2, 3)]


def add_up(parts):
    total = parts[0].astype(F32)
    for part in parts[1:]:
        total = total + part.astype(F32)
    return total


def scatter_sum(value, index, axis, shift):
    size = value.shape[0] // 4
    pieces = [lax.dynamic_slice_in_dim(value, ((index + k) & 3) * size, size) for k in range(4)]
    return add_up(exchange(pieces, axis, shift))


def gather_back(value, index, axis, shift):
    size = value.shape[0]
    full = jnp.zeros((4 * size, value.shape[1]), value.dtype)
    for k, piece in enumerate([value] + spread(value, axis, shift)):
        full = lax.dynamic_update_slice_in_dim(full, piece, ((index - k) & 3) * size, 0)
    return full


def sum_all(value, axis, shift):
    return add_up([value] + spread(value, axis, shift))


def node_part(features, cotangent, degree_wide, neighbour_sum, w_self, w_neigh):
    aggregate = (neighbour_sum / degree_wide).astype(BF16)
    preact = jnp.dot(features, w_self, preferred_element_type=F32) + jnp.dot(
        aggregate, w_neigh, preferred_element_type=F32
    )
    gate = jax.nn.sigmoid(preact)
    activations = (preact * gate).astype(BF16)
    slope = gate * (1.0 + preact * (1.0 - gate))
    dpreact = (cotangent.astype(F32) * slope).astype(BF16)
    dscaled = (
        jnp.einsum("ng,fg->nf", dpreact, w_neigh, preferred_element_type=F32) / degree_wide
    ).astype(BF16)
    return activations, aggregate, dpreact, dscaled


def per_device(
    features, w_self, w_neigh, cotangent, degree, tile_rows, tile_cols, tile_edges, tile_count
):
    nodes, width = features.shape
    row, col = lax.axis_index(ROW), lax.axis_index(COL)
    x, z, y = col & 3, col >> 2, row >> 2
    pos = jnp.stack([x, z, y, (row >> 1) & 1, row & 1]).astype(I32)

    with jax.named_scope("gather_features"):
        across = lax.ppermute(features, ROW, SWAP_Z)
        near = [features, across]
        for k in (1, 2, 3):
            near += [lax.ppermute(p, ROW, shift_y(k)) for p in (features, across)]
    lists = make_lists(pos, tile_count, tile_rows, tile_cols)
    tie = lax.optimization_barrier
    lists, near = tie((lists, near))
    with jax.named_scope("gather_features"):
        feature_pieces = near + [lax.ppermute(p, ROW, SWAP_CORE) for p in near]

    degree_wide = degree.astype(F32)[:, None]
    parts = [slice(0, nodes // 2), slice(nodes // 2, nodes)]

    def sum_along_x(pieces):
        with jax.named_scope("sum_along_x"):
            along_x = add_up(exchange(pieces, COL, shift_x))
            rounded = along_x.astype(BF16)
            size = along_x.shape[0] // 4
            return [along_x[:size]] + [rounded[k * size : (k + 1) * size] for k in (1, 2, 3)]

    def finish_nodes(by_z, mine):
        with jax.named_scope("sum_along_z"):
            neighbour_sum = add_up(exchange(by_z, COL, shift_z))
        return node_part(
            features[mine], cotangent[mine], degree_wide[mine], neighbour_sum, w_self, w_neigh
        )

    def gather_z(dscaled):
        with jax.named_scope("gather_dscaled"):
            return [dscaled] + spread(dscaled, COL, shift_z)

    def gather_x(from_z):
        with jax.named_scope("gather_dscaled"):
            line = jnp.concatenate(from_z)
            return [line] + spread(line, COL, shift_x)

    pieces_a = products(0, 4, lists, tile_edges, feature_pieces)
    pieces_a, lists, features, cotangent, degree_wide = tie(
        (pieces_a, lists, features, cotangent, degree_wide)
    )
    pieces_b = products(1, 4, lists, tile_edges, feature_pieces)
    by_z_a = sum_along_x(pieces_a)
    by_z_b = sum_along_x(pieces_b)
    act_a, aggregate_a, dpreact_a, dscaled_a = finish_nodes(by_z_a, parts[0])
    from_z_a, by_z_b = tie((gather_z(dscaled_a), by_z_b))
    gathered_a = gather_x(from_z_a)
    act_b, aggregate_b, dpreact_b, dscaled_b = finish_nodes(by_z_b, parts[1])
    from_z_b = gather_z(dscaled_b)
    gathered_b = gather_x(from_z_b)

    aggregate = jnp.concatenate([aggregate_a, aggregate_b])
    dpreact = jnp.concatenate([dpreact_a, dpreact_b])
    with jax.named_scope("weight_grads"):
        grads = jnp.concatenate(
            [
                jnp.einsum("nf,ng->fg", features, dpreact, preferred_element_type=F32),
                jnp.einsum("nf,ng->fg", aggregate, dpreact, preferred_element_type=F32),
            ]
        )
    grads, gathered_a = tie((grads, gathered_a))
    with jax.named_scope("weight_grads"):
        grads = scatter_sum(grads, y, ROW, shift_y)
        grads = grads + lax.ppermute(grads, ROW, SWAP_Z)
        grads = grads + lax.ppermute(grads, ROW, SWAP_CORE)
    sums_a = [
        products(2 + side, 1, lists, tile_edges, gathered_a, raw=True)[0] for side in (1, 0)
    ]
    sums_a, grads, gathered_b = tie((sums_a, grads, gathered_b))
    with jax.named_scope("weight_grads"):
        grads = sum_all(grads, COL, shift_x)
    [for_other] = products(5, 1, lists, tile_edges, gathered_b, first=sums_a[0])
    grads, for_other = tie((grads, for_other))
    from_other = lax.ppermute(for_other, ROW, SWAP_CORE)
    with jax.named_scope("weight_grads"):
        grads = sum_all(grads, COL, shift_z)
    [own] = products(4, 1, lists, tile_edges, gathered_b, first=sums_a[1])
    with jax.named_scope("sum_along_y"):
        both = add_up([own, from_other])
        size = both.shape[0] // 4
        by_y = [both[:size]] + [both[k * size : (k + 1) * size].astype(BF16) for k in (1, 2, 3)]
    with jax.named_scope("sum_along_y"):
        received = exchange(by_y, ROW, shift_y)
        along_y = add_up(received)
        for_across, along_y = along_y[nodes:].astype(BF16), along_y[:nodes]
    with jax.named_scope("sum_across_z"):
        neighbour_grad = along_y + lax.ppermute(for_across, ROW, SWAP_Z).astype(F32)
    with jax.named_scope("weight_grads"):
        grads = gather_back(grads, y, ROW, shift_y)
    own_grad = jnp.einsum("ng,fg->nf", dpreact, w_self, preferred_element_type=F32)
    feature_grad = (own_grad + neighbour_grad).astype(BF16)
    total_nodes = nodes * lax.axis_size(ROW) * lax.axis_size(COL)
    grads = grads * (1.0 / math.sqrt(total_nodes))
    return jnp.concatenate([act_a, act_b]), feature_grad, grads[:width], grads[width:]


def solution(mesh):
    by_device = P((ROW, COL))
    return jax.shard_map(
        per_device,
        mesh=mesh,
        in_specs=(
            P((ROW, COL), None),
            P(),
            P(),
            P((ROW, COL), None),
            by_device,
            by_device,
            by_device,
            P(None, (ROW, COL), None),
            by_device,
        ),
        out_specs=(P((ROW, COL), None), P((ROW, COL), None), P(), P()),
        check_vma=False,
    )
```

```python
import functools
import math

import jax
import jax.numpy as jnp
from jax import lax
from jax.experimental import pallas as pl
from jax.experimental.pallas import tpu as pltpu
from jax.sharding import PartitionSpec as P

F32, BF16, I32 = jnp.float32, jnp.bfloat16, jnp.int32
ROW, COL = "row", "col"
UNROLL = 8
VMEM_LIMIT = 32 << 20


def shift_x(k):
    return [(4 * z + x, 4 * z + (x + k) % 4) for z in range(4) for x in range(4)]


def shift_z(k):
    return [(4 * z + x, 4 * ((z + k) % 4) + x) for z in range(4) for x in range(4)]


def shift_y(k):
    return [(4 * y + i, 4 * ((y + k) % 4) + i) for y in range(4) for i in range(4)]


SWAP_Z = [(i, i ^ 2) for i in range(16)]
SWAP_CORE = [(i, i ^ 1) for i in range(16)]


LISTS = 6


def list_kernel(pos, count, rows, cols, slot, src, dst, counts):
    stretch = slot.shape[0] // LISTS
    x, z, y, zl, core = pos[0], pos[1], pos[2], pos[3], pos[4]
    for i in range(LISTS):
        counts[i] = 0

    def place(s, _):
        row, col = rows[s], cols[s]
        tile, chunk = row & 1, (row >> 1) & 1
        rx, rz = (row >> 2) & 3, row >> 4
        ccore, czl, cy = (col >> 2) & 1, (col >> 3) & 1, col >> 4
        other = ccore ^ core
        half = (czl ^ zl) * 4 + (col & 3)
        n = counts[chunk]
        counts[chunk] = n + 1
        at = chunk * stretch + n
        slot[at] = s
        src[at] = other * 32 + ((y - cy) & 3) * 8 + half
        dst[at] = ((rx - x) & 3) * 8 + ((rz - z) & 3) * 2 + tile
        which = 2 + 2 * chunk + other
        n = counts[which]
        counts[which] = n + 1
        at = which * stretch + n
        slot[at] = s
        src[at] = ((x - rx) & 3) * 8 + ((z - rz) & 3) * 2 + tile
        ky, kz, low = (cy - y) & 3, czl ^ zl, col & 1
        late = (col >> 1) & 1
        dst[at] = jnp.where(late == 0, ky * 4 + kz * 2 + low, 16 + kz * 8 + ky * 2 + low)
        return 0

    lax.fori_loop(0, count[0], place, 0)
    for i in range(LISTS):
        end = i * stretch + counts[i]
        for u in range(UNROLL):
            slot[end + u] = 0
            src[end + u] = 0
            dst[end + u] = 32


def make_lists(pos, count, rows, cols):
    smem = pl.BlockSpec(memory_space=pltpu.SMEM)
    length = LISTS * (rows.shape[0] + UNROLL)
    return pl.pallas_call(
        list_kernel,
        out_shape=[jax.ShapeDtypeStruct((length,), I32)] * 3 + [jax.ShapeDtypeStruct((8,), I32)],
        in_specs=[smem] * 4,
        out_specs=[smem] * 4,
        name="slot_lists",
    )(pos, count, rows, cols)


def edge_tile(edges, s):
    edge_count, _, tile = edges.shape
    column = lax.broadcasted_iota(I32, (tile, tile), 0).astype(F32).astype(BF16)
    one, zero = jnp.ones((tile, tile), BF16), jnp.zeros((tile, tile), BF16)
    total = None
    for k in range(edge_count):
        edge = jnp.broadcast_to(edges[k, pl.ds(s, 1), :], (16, tile)).astype(F32).astype(BF16)
        match = jnp.where(jnp.concatenate([edge] * (tile // 16), axis=0) == column, one, zero)
        total = match if total is None else total + match
    return total


def product_kernel(which, n_in, n_out, carried, raw, counts, slot, src, dst, edges, *refs):
    ins, refs = refs[:n_in], refs[n_in:]
    first, refs = (refs[0], refs[1:]) if carried else (None, refs)
    outs, refs = refs[:n_out], refs[n_out:]
    held, total, staged, in_sems, out_sems = refs
    tile, width = edges.shape[2], held.shape[1]
    n = counts[which]
    base = which * (src.shape[0] // LISTS)
    copies, at = [], 0
    for i, ref in enumerate(ins):
        size = ref.shape[0]
        copies.append(pltpu.make_async_copy(ref, held.at[pl.ds(at, size)], in_sems.at[i]))
        at += size
    results = total.shape[0] - tile
    if carried:
        copies.append(pltpu.make_async_copy(first, total.at[pl.ds(0, results)], in_sems.at[n_in]))
    for copy in copies:
        copy.start()
    if not carried:

        @pl.loop(0, results // tile)
        def _(i):
            total[pl.ds(pl.multiple_of(i * tile, tile), tile), :] = jnp.zeros((tile, width), F32)

    for copy in copies:
        copy.wait()
    over = ((0,), (0,)) if which < 2 else ((1,), (0,))

    @pl.loop(0, (n + UNROLL - 1) // UNROLL)
    def _(i):
        for half in range(0, UNROLL, 4):
            at = [base + i * UNROLL + half + u for u in range(4)]
            parts = [
                lax.dot_general(
                    edge_tile(edges, slot[p]),
                    held[pl.ds(pl.multiple_of(src[p] * tile, tile), tile), :],
                    (over, ((), ())),
                    preferred_element_type=F32,
                )
                for p in at
            ]
            for p, part in zip(at, parts):
                total[pl.ds(pl.multiple_of(dst[p] * tile, tile), tile), :] += part

    rows = results // n_out
    sends = []
    for o, ref in enumerate(outs):
        if raw:
            source = total.at[pl.ds(o * rows, rows)]
        else:
            source = staged.at[pl.ds(o * rows, rows)]

            @pl.loop(0, rows // tile)
            def _(i, o=o):
                part = pl.ds(pl.multiple_of(o * rows + i * tile, tile), tile)
                staged[part, :] = total[part, :].astype(BF16)

        sends.append(pltpu.make_async_copy(source, ref, out_sems.at[o]))
        sends[-1].start()
    for send in sends:
        send.wait()


def products(which, n_out, lists, edges, pieces, first=None, raw=False):
    slot, src, dst, counts = lists
    tile, width = edges.shape[2], pieces[0].shape[1]
    n_in, rows = len(pieces), sum(p.shape[0] for p in pieces)
    carried = first is not None
    smem, anywhere = pl.BlockSpec(memory_space=pltpu.SMEM), pl.BlockSpec(memory_space=pl.ANY)
    return pl.pallas_call(
        functools.partial(product_kernel, which, n_in, n_out, carried, raw),
        out_shape=[jax.ShapeDtypeStruct((32 * tile // n_out, width), F32 if raw else BF16)] * n_out,
        in_specs=[smem] * 4 + [pl.BlockSpec(memory_space=pltpu.VMEM)] + [anywhere] * (n_in + carried),
        out_specs=[anywhere] * n_out,
        scratch_shapes=[
            pltpu.VMEM((rows, width), BF16),
            pltpu.VMEM((33 * tile, width), F32),
            pltpu.VMEM((16, 128) if raw else (32 * tile, width), BF16),
            pltpu.SemaphoreType.DMA((n_in + 1,)),
            pltpu.SemaphoreType.DMA((n_out,)),
        ],
        compiler_params=pltpu.CompilerParams(vmem_limit_bytes=VMEM_LIMIT),
        cost_estimate=pl.CostEstimate(
            flops=128 * tile * tile * width * 2 * 4, bytes_accessed=12 << 20, transcendentals=0
        ),
        name="tile_products",
    )(counts, slot, src, dst, edges, *pieces, *([first] if carried else []))


def spread(value, axis, shift):
    return [lax.ppermute(value, axis, shift(k)) for k in (1, 2, 3)]


def exchange(pieces, axis, shift):
    return [pieces[0]] + [lax.ppermute(pieces[k], axis, shift(k)) for k in (1, 2, 3)]


def add_up(parts):
    total = parts[0].astype(F32)
    for part in parts[1:]:
        total = total + part.astype(F32)
    return total


def after(value, *events):
    return lax.optimization_barrier((value, events))[0]


def swap(value, axis, bit):
    return lax.ppermute(value, axis, [(i, i ^ bit) for i in range(16)])


def halve(value, axis, bit, set_here):
    size = value.shape[0] // 2
    kept = lax.dynamic_slice_in_dim(value, set_here * size, size)
    return kept + swap(lax.dynamic_slice_in_dim(value, (1 - set_here) * size, size), axis, bit)


def join(value, axis, bit, set_here):
    other = swap(value, axis, bit)
    return jnp.where(
        set_here == 0, jnp.concatenate([value, other]), jnp.concatenate([other, value])
    )


def node_part(features, cotangent, degree_wide, neighbour_sum, w_self, w_neigh):
    aggregate = (neighbour_sum / degree_wide).astype(BF16)
    preact = jnp.dot(features, w_self, preferred_element_type=F32) + jnp.dot(
        aggregate, w_neigh, preferred_element_type=F32
    )
    gate = jax.nn.sigmoid(preact)
    activations = (preact * gate).astype(BF16)
    slope = gate * (1.0 + preact * (1.0 - gate))
    dpreact = (cotangent.astype(F32) * slope).astype(BF16)
    dscaled = (
        jnp.einsum("ng,fg->nf", dpreact, w_neigh, preferred_element_type=F32) / degree_wide
    ).astype(BF16)
    return activations, aggregate, dpreact, dscaled


def per_device(
    features, w_self, w_neigh, cotangent, degree, tile_rows, tile_cols, tile_edges, tile_count
):
    nodes, width = features.shape
    row, col = lax.axis_index(ROW), lax.axis_index(COL)
    x, z, y = col & 3, col >> 2, row >> 2
    pos = jnp.stack([x, z, y, (row >> 1) & 1, row & 1]).astype(I32)

    with jax.named_scope("gather_features"):
        across = lax.ppermute(features, ROW, SWAP_Z)
        near = [features, across]
        for k in (1, 2, 3):
            near += [lax.ppermute(p, ROW, shift_y(k)) for p in (features, across)]
    lists = make_lists(pos, tile_count, tile_rows, tile_cols)
    near = after(near, lists)
    with jax.named_scope("gather_features"):
        feature_pieces = near + [lax.ppermute(p, ROW, SWAP_CORE) for p in near]

    degree_wide = degree.astype(F32)[:, None]
    parts = [slice(0, nodes // 2), slice(nodes // 2, nodes)]

    def split_by_z(received):
        with jax.named_scope("sum_along_x"):
            along_x = add_up(received)
            rounded = along_x.astype(BF16)
            size = along_x.shape[0] // 4
            return [along_x[:size]] + [rounded[k * size : (k + 1) * size] for k in (1, 2, 3)]

    def finish_nodes(by_z, mine, *events):
        with jax.named_scope("sum_along_z"):
            neighbour_sum = add_up(after(exchange(by_z, COL, shift_z), *events))
        return node_part(
            features[mine], cotangent[mine], degree_wide[mine], neighbour_sum, w_self, w_neigh
        )

    def gather_z(dscaled):
        with jax.named_scope("gather_dscaled"):
            return [dscaled] + spread(dscaled, COL, shift_z)

    def gather_x(from_z):
        with jax.named_scope("gather_dscaled"):
            line = jnp.concatenate(from_z)
            return [line] + spread(line, COL, shift_x)

    pieces_a = products(0, 4, lists, tile_edges, feature_pieces)
    lists, features, cotangent, degree_wide = after(
        (lists, features, cotangent, degree_wide), pieces_a
    )
    pieces_b = products(1, 4, lists, tile_edges, feature_pieces)
    with jax.named_scope("sum_along_x"):
        received_a = exchange(pieces_a, COL, shift_x)
        received_b = exchange(after(pieces_b, received_a[1]), COL, shift_x)
    by_z_a, by_z_b = split_by_z(received_a), split_by_z(received_b)
    act_a, aggregate_a, dpreact_a, dscaled_a = finish_nodes(by_z_a, parts[0])
    from_z_a = gather_z(dscaled_a)
    gathered_a = gather_x(from_z_a)
    act_b, aggregate_b, dpreact_b, dscaled_b = finish_nodes(
        after(by_z_b, from_z_a), parts[1], gathered_a[1]
    )
    aggregate = jnp.concatenate([aggregate_a, aggregate_b])
    dpreact = jnp.concatenate([dpreact_a, dpreact_b])
    with jax.named_scope("weight_grads"):
        grads = jnp.concatenate(
            [
                jnp.einsum("nf,ng->fg", features, dpreact, preferred_element_type=F32),
                jnp.einsum("nf,ng->fg", aggregate, dpreact, preferred_element_type=F32),
            ]
        )
        grads = halve(grads, ROW, 8, y >> 1)
    gathered_b = gather_x(after(gather_z(dscaled_b), gathered_a, grads))
    with jax.named_scope("weight_grads"):
        grads = halve(grads, ROW, 4, y & 1)
        grads = grads + swap(grads, COL, 1)
        grads = grads + swap(grads, COL, 2)
    sums_a = [
        products(2 + side, 1, lists, tile_edges, gathered_a, raw=True)[0] for side in (1, 0)
    ]
    gathered_b = after(gathered_b, sums_a, grads)
    with jax.named_scope("weight_grads"):
        grads = after(grads, gathered_b)
        grads = grads + swap(grads, COL, 4)
    [for_other] = products(5, 1, lists, tile_edges, gathered_b, first=sums_a[0])
    from_other = lax.ppermute(for_other, ROW, SWAP_CORE)
    with jax.named_scope("weight_grads"):
        grads = after(grads, for_other)
        grads = grads + swap(grads, COL, 8)
    [own] = products(4, 1, lists, tile_edges, gathered_b, first=sums_a[1])
    half = own.shape[0] // 2
    with jax.named_scope("sum_early"):
        both = add_up([own[:half], from_other[:half]])
        size = half // 4
        by_y = [both[:size]] + [both[k * size : (k + 1) * size].astype(BF16) for k in (1, 2, 3)]
        received = exchange(by_y, ROW, shift_y)
        along_y = add_up(received)
        size //= 2
        early = along_y[:size] + lax.ppermute(along_y[size:].astype(BF16), ROW, SWAP_Z).astype(F32)
    with jax.named_scope("sum_late"):
        both = add_up([own[half:], from_other[half:]])
        across_z = both[: half // 2] + lax.ppermute(
            both[half // 2 :].astype(BF16), ROW, SWAP_Z
        ).astype(F32)
        by_y = [across_z[:size]]
        by_y += [across_z[k * size : (k + 1) * size].astype(BF16) for k in (1, 2, 3)]
        late = add_up(exchange(by_y, ROW, shift_y))
    neighbour_grad = jnp.concatenate([early, late])
    with jax.named_scope("weight_grads"):
        grads = after(grads, own)
        grads = grads + swap(grads, ROW, 2)
        grads = after(grads, received[1])
        grads = grads + swap(grads, ROW, 1)
        grads = join(after(grads, along_y), ROW, 4, y & 1)
        grads = join(grads, ROW, 8, y >> 1)
    own_grad = jnp.einsum("ng,fg->nf", dpreact, w_self, preferred_element_type=F32)
    feature_grad = (own_grad + neighbour_grad).astype(BF16)
    total_nodes = nodes * lax.axis_size(ROW) * lax.axis_size(COL)
    grads = grads * (1.0 / math.sqrt(total_nodes))
    return jnp.concatenate([act_a, act_b]), feature_grad, grads[:width], grads[width:]


def solution(mesh):
    by_device = P((ROW, COL))
    return jax.shard_map(
        per_device,
        mesh=mesh,
        in_specs=(
            P((ROW, COL), None),
            P(),
            P(),
            P((ROW, COL), None),
            by_device,
            by_device,
            by_device,
            P(None, (ROW, COL), None),
            by_device,
        ),
        out_specs=(P((ROW, COL), None), P((ROW, COL), None), P(), P()),
        check_vma=False,
    )
```

```python
import functools
import math

import jax
import jax.numpy as jnp
from jax import lax
from jax.experimental import pallas as pl
from jax.experimental.pallas import tpu as pltpu
from jax.sharding import PartitionSpec as P

F32, BF16, I32 = jnp.float32, jnp.bfloat16, jnp.int32
ROW, COL = "row", "col"
UNROLL = 8
FORWARD_VMEM, BACKWARD_VMEM = 56 << 20, 32 << 20


def shift_x(k):
    return [(4 * z + x, 4 * z + (x + k) % 4) for z in range(4) for x in range(4)]


def shift_z(k):
    return [(4 * z + x, 4 * ((z + k) % 4) + x) for z in range(4) for x in range(4)]


def shift_y(k):
    return [(4 * y + i, 4 * ((y + k) % 4) + i) for y in range(4) for i in range(4)]


SWAP_Z = [(i, i ^ 2) for i in range(16)]
SWAP_CORE = [(i, i ^ 1) for i in range(16)]


LISTS = 6


def list_kernel(pos, count, rows, cols, slot, src, dst, counts):
    stretch = slot.shape[0] // LISTS
    x, z, y, zl, core = pos[0], pos[1], pos[2], pos[3], pos[4]
    for i in range(LISTS):
        counts[i] = 0

    def place(s, _):
        row, col = rows[s], cols[s]
        tile, chunk = row & 1, (row >> 1) & 1
        rx, rz = (row >> 2) & 3, row >> 4
        ccore, czl, cy = (col >> 2) & 1, (col >> 3) & 1, col >> 4
        other = ccore ^ core
        half = (czl ^ zl) * 4 + (col & 3)
        n = counts[chunk]
        counts[chunk] = n + 1
        at = chunk * stretch + n
        slot[at] = s
        src[at] = other * 32 + ((y - cy) & 3) * 8 + half
        dst[at] = ((rx - x) & 3) * 8 + ((rz - z) & 3) * 2 + tile
        which = 2 + 2 * chunk + other
        n = counts[which]
        counts[which] = n + 1
        at = which * stretch + n
        slot[at] = s
        src[at] = ((x - rx) & 3) * 8 + ((z - rz) & 3) * 2 + tile
        ky, kz, low = (cy - y) & 3, czl ^ zl, col & 1
        late = (col >> 1) & 1
        dst[at] = jnp.where(late == 0, ky * 4 + kz * 2 + low, 16 + kz * 8 + ky * 2 + low)
        return 0

    lax.fori_loop(0, count[0], place, 0)
    for i in range(LISTS):
        end = i * stretch + counts[i]
        for u in range(UNROLL):
            slot[end + u] = 0
            src[end + u] = 0
            dst[end + u] = 32


def make_lists(pos, count, rows, cols):
    smem = pl.BlockSpec(memory_space=pltpu.SMEM)
    length = LISTS * (rows.shape[0] + UNROLL)
    return pl.pallas_call(
        list_kernel,
        out_shape=[jax.ShapeDtypeStruct((length,), I32)] * 3 + [jax.ShapeDtypeStruct((8,), I32)],
        in_specs=[smem] * 4,
        out_specs=[smem] * 4,
        name="slot_lists",
    )(pos, count, rows, cols)


def edge_tile(edges, s):
    edge_count, _, tile = edges.shape
    column = lax.broadcasted_iota(I32, (tile, tile), 0).astype(F32).astype(BF16)
    one, zero = jnp.ones((tile, tile), BF16), jnp.zeros((tile, tile), BF16)
    total = None
    for k in range(edge_count):
        edge = jnp.broadcast_to(edges[k, pl.ds(s, 1), :], (16, tile)).astype(F32).astype(BF16)
        match = jnp.where(jnp.concatenate([edge] * (tile // 16), axis=0) == column, one, zero)
        total = match if total is None else total + match
    return total


def product_kernel(which, n_in, n_out, carried, raw, counts, slot, src, dst, edges, *refs):
    ins, refs = refs[:n_in], refs[n_in:]
    first, refs = (refs[0], refs[1:]) if carried else (None, refs)
    outs, refs = refs[:n_out], refs[n_out:]
    held, total, staged, in_sems, out_sems = refs
    tile, width = edges.shape[2], held.shape[1]
    n = counts[which]
    base = which * (src.shape[0] // LISTS)
    copies, at = [], 0
    for i, ref in enumerate(ins):
        size = ref.shape[0]
        copies.append(pltpu.make_async_copy(ref, held.at[pl.ds(at, size)], in_sems.at[i]))
        at += size
    results = total.shape[0] - tile
    if carried:
        copies.append(pltpu.make_async_copy(first, total.at[pl.ds(0, results)], in_sems.at[n_in]))
    for copy in copies:
        copy.start()
    if not carried:

        @pl.loop(0, results // tile)
        def _(i):
            total[pl.ds(pl.multiple_of(i * tile, tile), tile), :] = jnp.zeros((tile, width), F32)

    for copy in copies:
        copy.wait()
    over = ((0,), (0,)) if which < 2 else ((1,), (0,))

    @pl.loop(0, (n + UNROLL - 1) // UNROLL)
    def _(i):
        for half in range(0, UNROLL, 4):
            at = [base + i * UNROLL + half + u for u in range(4)]
            parts = [
                lax.dot_general(
                    edge_tile(edges, slot[p]),
                    held[pl.ds(pl.multiple_of(src[p] * tile, tile), tile), :],
                    (over, ((), ())),
                    preferred_element_type=F32,
                )
                for p in at
            ]
            for p, part in zip(at, parts):
                total[pl.ds(pl.multiple_of(dst[p] * tile, tile), tile), :] += part

    rows = results // n_out
    sends = []
    for o, ref in enumerate(outs):
        if raw:
            source = total.at[pl.ds(o * rows, rows)]
        else:
            source = staged.at[pl.ds(o * rows, rows)]

            @pl.loop(0, rows // tile)
            def _(i, o=o):
                part = pl.ds(pl.multiple_of(o * rows + i * tile, tile), tile)
                staged[part, :] = total[part, :].astype(BF16)

        sends.append(pltpu.make_async_copy(source, ref, out_sems.at[o]))
        sends[-1].start()
    for send in sends:
        send.wait()


def products(which, n_out, lists, edges, pieces, first=None, raw=False):
    slot, src, dst, counts = lists
    tile, width = edges.shape[2], pieces[0].shape[1]
    n_in, rows = len(pieces), sum(p.shape[0] for p in pieces)
    carried = first is not None
    smem, anywhere = pl.BlockSpec(memory_space=pltpu.SMEM), pl.BlockSpec(memory_space=pl.ANY)
    return pl.pallas_call(
        functools.partial(product_kernel, which, n_in, n_out, carried, raw),
        out_shape=[jax.ShapeDtypeStruct((32 * tile // n_out, width), F32 if raw else BF16)] * n_out,
        in_specs=[smem] * 4 + [pl.BlockSpec(memory_space=pltpu.VMEM)] + [anywhere] * (n_in + carried),
        out_specs=[anywhere] * n_out,
        scratch_shapes=[
            pltpu.VMEM((rows, width), BF16),
            pltpu.VMEM((33 * tile, width), F32),
            pltpu.VMEM((16, 128) if raw else (32 * tile, width), BF16),
            pltpu.SemaphoreType.DMA((n_in + 1,)),
            pltpu.SemaphoreType.DMA((n_out,)),
        ],
        compiler_params=pltpu.CompilerParams(
            vmem_limit_bytes=FORWARD_VMEM if which < 2 else BACKWARD_VMEM
        ),
        cost_estimate=pl.CostEstimate(
            flops=128 * tile * tile * width * 2 * 4, bytes_accessed=12 << 20, transcendentals=0
        ),
        name="tile_products",
    )(counts, slot, src, dst, edges, *pieces, *([first] if carried else []))


def spread(value, axis, shift):
    return [lax.ppermute(value, axis, shift(k)) for k in (1, 2, 3)]


def exchange(pieces, axis, shift):
    return [pieces[0]] + [lax.ppermute(pieces[k], axis, shift(k)) for k in (1, 2, 3)]


def add_up(parts):
    total = parts[0].astype(F32)
    for part in parts[1:]:
        total = total + part.astype(F32)
    return total


def after(value, *events):
    return lax.optimization_barrier((value, events))[0]


def swap(value, axis, bit):
    return lax.ppermute(value, axis, [(i, i ^ bit) for i in range(16)])


def halve(value, axis, bit, set_here):
    size = value.shape[0] // 2
    kept = lax.dynamic_slice_in_dim(value, set_here * size, size)
    return kept + swap(lax.dynamic_slice_in_dim(value, (1 - set_here) * size, size), axis, bit)


def join(value, axis, bit, set_here):
    other = swap(value, axis, bit)
    return jnp.where(
        set_here == 0, jnp.concatenate([value, other]), jnp.concatenate([other, value])
    )


def node_part(features, cotangent, degree_wide, neighbour_sum, w_self, w_neigh):
    aggregate = (neighbour_sum / degree_wide).astype(BF16)
    preact = jnp.dot(features, w_self, preferred_element_type=F32) + jnp.dot(
        aggregate, w_neigh, preferred_element_type=F32
    )
    gate = jax.nn.sigmoid(preact)
    activations = (preact * gate).astype(BF16)
    slope = gate * (1.0 + preact * (1.0 - gate))
    dpreact = (cotangent.astype(F32) * slope).astype(BF16)
    dscaled = (
        jnp.einsum("ng,fg->nf", dpreact, w_neigh, preferred_element_type=F32) / degree_wide
    ).astype(BF16)
    return activations, aggregate, dpreact, dscaled


def per_device(
    features, w_self, w_neigh, cotangent, degree, tile_rows, tile_cols, tile_edges, tile_count
):
    nodes, width = features.shape
    row, col = lax.axis_index(ROW), lax.axis_index(COL)
    x, z, y = col & 3, col >> 2, row >> 2
    pos = jnp.stack([x, z, y, (row >> 1) & 1, row & 1]).astype(I32)

    with jax.named_scope("gather_features"):
        across = lax.ppermute(features, ROW, SWAP_Z)
        near = [features, across]
        for k in (1, 2, 3):
            near += [lax.ppermute(p, ROW, shift_y(k)) for p in (features, across)]
    lists = make_lists(pos, tile_count, tile_rows, tile_cols)
    near = after(near, lists)
    with jax.named_scope("gather_features"):
        feature_pieces = near + [lax.ppermute(p, ROW, SWAP_CORE) for p in near]

    degree_wide = degree.astype(F32)[:, None]
    parts = [slice(0, nodes // 2), slice(nodes // 2, nodes)]

    def split_by_z(received):
        with jax.named_scope("sum_along_x"):
            along_x = add_up(received)
            rounded = along_x.astype(BF16)
            size = along_x.shape[0] // 4
            return [along_x[:size]] + [rounded[k * size : (k + 1) * size] for k in (1, 2, 3)]

    def finish_nodes(by_z, mine, *events):
        with jax.named_scope("sum_along_z"):
            neighbour_sum = add_up(after(exchange(by_z, COL, shift_z), *events))
        return node_part(
            features[mine], cotangent[mine], degree_wide[mine], neighbour_sum, w_self, w_neigh
        )

    def gather_z(dscaled):
        with jax.named_scope("gather_dscaled"):
            return [dscaled] + spread(dscaled, COL, shift_z)

    def gather_x(from_z):
        with jax.named_scope("gather_dscaled"):
            line = jnp.concatenate(from_z)
            return [line] + spread(line, COL, shift_x)

    pieces_a = products(0, 4, lists, tile_edges, feature_pieces)
    lists, features, cotangent, degree_wide = after(
        (lists, features, cotangent, degree_wide), pieces_a
    )
    pieces_b = products(1, 4, lists, tile_edges, feature_pieces)
    with jax.named_scope("sum_along_x"):
        received_a = exchange(pieces_a, COL, shift_x)
        received_b = exchange(after(pieces_b, received_a[1]), COL, shift_x)
    by_z_a, by_z_b = split_by_z(received_a), split_by_z(received_b)
    act_a, aggregate_a, dpreact_a, dscaled_a = finish_nodes(by_z_a, parts[0])
    from_z_a = gather_z(dscaled_a)
    gathered_a = gather_x(from_z_a)
    act_b, aggregate_b, dpreact_b, dscaled_b = finish_nodes(by_z_b, parts[1], from_z_a)
    from_z_b = gather_z(dscaled_b)
    aggregate = jnp.concatenate([aggregate_a, aggregate_b])
    dpreact = jnp.concatenate([dpreact_a, dpreact_b])
    features, aggregate = after((features, aggregate), from_z_b[1])
    with jax.named_scope("weight_grads"):
        grads = jnp.concatenate(
            [
                jnp.einsum("nf,ng->fg", features, dpreact, preferred_element_type=F32),
                jnp.einsum("nf,ng->fg", aggregate, dpreact, preferred_element_type=F32),
            ]
        )
    gathered_b = gather_x(after(from_z_b, gathered_a))
    with jax.named_scope("weight_grads"):
        grads = halve(grads, ROW, 8, y >> 1)
        grads = halve(grads, ROW, 4, y & 1)
        grads = grads + swap(grads, COL, 4)
    sums_a = [
        products(2 + side, 1, lists, tile_edges, gathered_a, raw=True)[0] for side in (1, 0)
    ]
    gathered_b = after(gathered_b, sums_a, grads)
    with jax.named_scope("weight_grads"):
        grads = after(grads, gathered_b)
        grads = grads + swap(grads, COL, 8)
    [for_other] = products(5, 1, lists, tile_edges, gathered_b, first=sums_a[0])
    from_other = lax.ppermute(for_other, ROW, SWAP_CORE)
    with jax.named_scope("weight_grads"):
        grads = after(grads, for_other)
        grads = grads + swap(grads, COL, 1)
    [own] = products(4, 1, lists, tile_edges, gathered_b, first=sums_a[1])
    half = own.shape[0] // 2
    with jax.named_scope("sum_early"):
        both = add_up([own[:half], from_other[:half]])
        size = half // 4
        by_y = [both[:size]] + [both[k * size : (k + 1) * size].astype(BF16) for k in (1, 2, 3)]
        received = exchange(by_y, ROW, shift_y)
        along_y = add_up(received)
        size //= 2
        early = along_y[:size] + lax.ppermute(along_y[size:].astype(BF16), ROW, SWAP_Z).astype(F32)
    with jax.named_scope("sum_late"):
        both = add_up([own[half:], from_other[half:]])
        across_z = both[: half // 2] + lax.ppermute(
            both[half // 2 :].astype(BF16), ROW, SWAP_Z
        ).astype(F32)
        by_y = [across_z[:size]]
        by_y += [across_z[k * size : (k + 1) * size].astype(BF16) for k in (1, 2, 3)]
        late = add_up(exchange(by_y, ROW, shift_y))
    neighbour_grad = jnp.concatenate([early, late])
    with jax.named_scope("weight_grads"):
        grads = after(grads, own)
        grads = grads + swap(grads, COL, 2)
        grads = after(grads, received[1])
        grads = grads + swap(grads, ROW, 1)
        grads = after(grads, along_y)
        grads = grads + swap(grads, ROW, 2)
        grads = join(grads, ROW, 4, y & 1)
        grads = join(grads, ROW, 8, y >> 1)
    own_grad = jnp.einsum("ng,fg->nf", dpreact, w_self, preferred_element_type=F32)
    feature_grad = (own_grad + neighbour_grad).astype(BF16)
    total_nodes = nodes * lax.axis_size(ROW) * lax.axis_size(COL)
    grads = grads * (1.0 / math.sqrt(total_nodes))
    return jnp.concatenate([act_a, act_b]), feature_grad, grads[:width], grads[width:]


def solution(mesh):
    by_device = P((ROW, COL))
    return jax.shard_map(
        per_device,
        mesh=mesh,
        in_specs=(
            P((ROW, COL), None),
            P(),
            P(),
            P((ROW, COL), None),
            by_device,
            by_device,
            by_device,
            P(None, (ROW, COL), None),
            by_device,
        ),
        out_specs=(P((ROW, COL), None), P((ROW, COL), None), P(), P()),
        check_vma=False,
    )
```

```python
import functools
import math

import jax
import jax.numpy as jnp
from jax import lax
from jax.experimental import pallas as pl
from jax.experimental.pallas import tpu as pltpu
from jax.sharding import PartitionSpec as P

F32, BF16, I32 = jnp.float32, jnp.bfloat16, jnp.int32
ROW, COL = "row", "col"
UNROLL = 8
FORWARD_VMEM, BACKWARD_VMEM = 56 << 20, 32 << 20


def shift_x(k):
    return [(4 * z + x, 4 * z + (x + k) % 4) for z in range(4) for x in range(4)]


def shift_z(k):
    return [(4 * z + x, 4 * ((z + k) % 4) + x) for z in range(4) for x in range(4)]


def shift_y(k):
    return [(4 * y + i, 4 * ((y + k) % 4) + i) for y in range(4) for i in range(4)]


SWAP_Z = [(i, i ^ 2) for i in range(16)]
SWAP_CORE = [(i, i ^ 1) for i in range(16)]


LISTS = 6


def list_kernel(pos, count, rows, cols, slot, src, dst, counts):
    stretch = slot.shape[0] // LISTS
    x, z, y, zl, core = pos[0], pos[1], pos[2], pos[3], pos[4]
    for i in range(LISTS):
        counts[i] = 0

    def place(s, _):
        row, col = rows[s], cols[s]
        tile, chunk = row & 1, (row >> 1) & 1
        rx, rz = (row >> 2) & 3, row >> 4
        ccore, czl, cy = (col >> 2) & 1, (col >> 3) & 1, col >> 4
        other = ccore ^ core
        half = (czl ^ zl) * 4 + (col & 3)
        n = counts[chunk]
        counts[chunk] = n + 1
        at = chunk * stretch + n
        slot[at] = s
        src[at] = other * 32 + ((y - cy) & 3) * 8 + half
        dst[at] = ((rx - x) & 3) * 8 + ((rz - z) & 3) * 2 + tile
        which = 2 + 2 * chunk + other
        n = counts[which]
        counts[which] = n + 1
        at = which * stretch + n
        slot[at] = s
        src[at] = ((x - rx) & 3) * 8 + ((z - rz) & 3) * 2 + tile
        ky, kz, low = (cy - y) & 3, czl ^ zl, col & 1
        late = (col >> 1) & 1
        dst[at] = jnp.where(late == 0, ky * 4 + kz * 2 + low, 16 + kz * 8 + ky * 2 + low)
        return 0

    lax.fori_loop(0, count[0], place, 0)
    for i in range(LISTS):
        end = i * stretch + counts[i]
        for u in range(UNROLL):
            slot[end + u] = 0
            src[end + u] = 0
            dst[end + u] = 32


def make_lists(pos, count, rows, cols):
    smem = pl.BlockSpec(memory_space=pltpu.SMEM)
    length = LISTS * (rows.shape[0] + UNROLL)
    return pl.pallas_call(
        list_kernel,
        out_shape=[jax.ShapeDtypeStruct((length,), I32)] * 3 + [jax.ShapeDtypeStruct((8,), I32)],
        in_specs=[smem] * 4,
        out_specs=[smem] * 4,
        name="slot_lists",
    )(pos, count, rows, cols)


def edge_tile(edges, s):
    edge_count, _, tile = edges.shape
    column = lax.broadcasted_iota(I32, (tile, tile), 0).astype(F32).astype(BF16)
    one, zero = jnp.ones((tile, tile), BF16), jnp.zeros((tile, tile), BF16)
    total = None
    for k in range(edge_count):
        edge = jnp.broadcast_to(edges[k, pl.ds(s, 1), :], (16, tile)).astype(F32).astype(BF16)
        match = jnp.where(jnp.concatenate([edge] * (tile // 16), axis=0) == column, one, zero)
        total = match if total is None else total + match
    return total


def product_kernel(which, n_in, n_out, carried, raw, counts, slot, src, dst, edges, *refs):
    ins, refs = refs[:n_in], refs[n_in:]
    first, refs = (refs[0], refs[1:]) if carried else (None, refs)
    outs, refs = refs[:n_out], refs[n_out:]
    held, total, staged, in_sems, out_sems = refs
    tile, width = edges.shape[2], held.shape[1]
    n = counts[which]
    base = which * (src.shape[0] // LISTS)
    copies, at = [], 0
    for i, ref in enumerate(ins):
        size = ref.shape[0]
        copies.append(pltpu.make_async_copy(ref, held.at[pl.ds(at, size)], in_sems.at[i]))
        at += size
    results = total.shape[0] - tile
    if carried:
        copies.append(pltpu.make_async_copy(first, total.at[pl.ds(0, results)], in_sems.at[n_in]))
    for copy in copies:
        copy.start()
    if not carried:

        @pl.loop(0, results // tile)
        def _(i):
            total[pl.ds(pl.multiple_of(i * tile, tile), tile), :] = jnp.zeros((tile, width), F32)

    for copy in copies:
        copy.wait()
    over = ((0,), (0,)) if which < 2 else ((1,), (0,))

    @pl.loop(0, (n + UNROLL - 1) // UNROLL)
    def _(i):
        for half in range(0, UNROLL, 4):
            at = [base + i * UNROLL + half + u for u in range(4)]
            parts = [
                lax.dot_general(
                    edge_tile(edges, slot[p]),
                    held[pl.ds(pl.multiple_of(src[p] * tile, tile), tile), :],
                    (over, ((), ())),
                    preferred_element_type=F32,
                )
                for p in at
            ]
            for p, part in zip(at, parts):
                total[pl.ds(pl.multiple_of(dst[p] * tile, tile), tile), :] += part

    rows = results // n_out
    sends = []
    for o, ref in enumerate(outs):
        if raw:
            source = total.at[pl.ds(o * rows, rows)]
        else:
            source = staged.at[pl.ds(o * rows, rows)]

            @pl.loop(0, rows // tile)
            def _(i, o=o):
                part = pl.ds(pl.multiple_of(o * rows + i * tile, tile), tile)
                staged[part, :] = total[part, :].astype(BF16)

        sends.append(pltpu.make_async_copy(source, ref, out_sems.at[o]))
        sends[-1].start()
    for send in sends:
        send.wait()


def products(which, n_out, lists, edges, pieces, first=None, raw=False):
    slot, src, dst, counts = lists
    tile, width = edges.shape[2], pieces[0].shape[1]
    n_in, rows = len(pieces), sum(p.shape[0] for p in pieces)
    carried = first is not None
    smem, anywhere = pl.BlockSpec(memory_space=pltpu.SMEM), pl.BlockSpec(memory_space=pl.ANY)
    return pl.pallas_call(
        functools.partial(product_kernel, which, n_in, n_out, carried, raw),
        out_shape=[jax.ShapeDtypeStruct((32 * tile // n_out, width), F32 if raw else BF16)] * n_out,
        in_specs=[smem] * 4 + [pl.BlockSpec(memory_space=pltpu.VMEM)] + [anywhere] * (n_in + carried),
        out_specs=[anywhere] * n_out,
        scratch_shapes=[
            pltpu.VMEM((rows, width), BF16),
            pltpu.VMEM((33 * tile, width), F32),
            pltpu.VMEM((16, 128) if raw else (32 * tile, width), BF16),
            pltpu.SemaphoreType.DMA((n_in + 1,)),
            pltpu.SemaphoreType.DMA((n_out,)),
        ],
        compiler_params=pltpu.CompilerParams(
            vmem_limit_bytes=FORWARD_VMEM if which < 2 else BACKWARD_VMEM
        ),
        cost_estimate=pl.CostEstimate(
            flops=128 * tile * tile * width * 2 * 4, bytes_accessed=12 << 20, transcendentals=0
        ),
        name="tile_products",
    )(counts, slot, src, dst, edges, *pieces, *([first] if carried else []))


def spread(value, axis, shift):
    return [lax.ppermute(value, axis, shift(k)) for k in (1, 2, 3)]


def exchange(pieces, axis, shift):
    return [pieces[0]] + [lax.ppermute(pieces[k], axis, shift(k)) for k in (1, 2, 3)]


def add_up(parts):
    total = parts[0].astype(F32)
    for part in parts[1:]:
        total = total + part.astype(F32)
    return total


def after(value, *events):
    return lax.optimization_barrier((value, events))[0]


def swap(value, axis, bit):
    return lax.ppermute(value, axis, [(i, i ^ bit) for i in range(16)])


def halve(value, axis, bit, set_here):
    size = value.shape[0] // 2
    kept = lax.dynamic_slice_in_dim(value, set_here * size, size)
    return kept + swap(lax.dynamic_slice_in_dim(value, (1 - set_here) * size, size), axis, bit)


def join(value, axis, bit, set_here):
    other = swap(value, axis, bit)
    return jnp.where(
        set_here == 0, jnp.concatenate([value, other]), jnp.concatenate([other, value])
    )


def node_part(features, cotangent, degree_wide, neighbour_sum, w_self, w_neigh):
    aggregate = (neighbour_sum / degree_wide).astype(BF16)
    preact = jnp.dot(features, w_self, preferred_element_type=F32) + jnp.dot(
        aggregate, w_neigh, preferred_element_type=F32
    )
    gate = jax.nn.sigmoid(preact)
    activations = (preact * gate).astype(BF16)
    slope = gate * (1.0 + preact * (1.0 - gate))
    dpreact = (cotangent.astype(F32) * slope).astype(BF16)
    dscaled = (
        jnp.einsum("ng,fg->nf", dpreact, w_neigh, preferred_element_type=F32) / degree_wide
    ).astype(BF16)
    return activations, aggregate, dpreact, dscaled


def per_device(
    features, w_self, w_neigh, cotangent, degree, tile_rows, tile_cols, tile_edges, tile_count
):
    nodes, width = features.shape
    row, col = lax.axis_index(ROW), lax.axis_index(COL)
    x, z, y = col & 3, col >> 2, row >> 2
    pos = jnp.stack([x, z, y, (row >> 1) & 1, row & 1]).astype(I32)

    with jax.named_scope("gather_features"):
        across = lax.ppermute(features, ROW, SWAP_Z)
        near = [features, across]
        for k in (1, 2, 3):
            near += [lax.ppermute(p, ROW, shift_y(k)) for p in (features, across)]
    lists = make_lists(pos, tile_count, tile_rows, tile_cols)
    near = after(near, lists)
    with jax.named_scope("gather_features"):
        feature_pieces = near + [lax.ppermute(p, ROW, SWAP_CORE) for p in near]

    degree_wide = degree.astype(F32)[:, None]
    parts = [slice(0, nodes // 2), slice(nodes // 2, nodes)]

    def split_by_z(received):
        with jax.named_scope("sum_along_x"):
            along_x = add_up(received)
            rounded = along_x.astype(BF16)
            size = along_x.shape[0] // 4
            return [along_x[:size]] + [rounded[k * size : (k + 1) * size] for k in (1, 2, 3)]

    def finish_nodes(by_z, mine, *events):
        with jax.named_scope("sum_along_z"):
            neighbour_sum = add_up(after(exchange(by_z, COL, shift_z), *events))
        return node_part(
            features[mine], cotangent[mine], degree_wide[mine], neighbour_sum, w_self, w_neigh
        )

    def gather_z(dscaled):
        with jax.named_scope("gather_dscaled"):
            return [dscaled] + spread(dscaled, COL, shift_z)

    def gather_x(from_z):
        with jax.named_scope("gather_dscaled"):
            line = jnp.concatenate(from_z)
            return [line] + spread(line, COL, shift_x)

    pieces_a = products(0, 4, lists, tile_edges, feature_pieces)
    lists, features, cotangent, degree_wide = after(
        (lists, features, cotangent, degree_wide), pieces_a
    )
    pieces_b = products(1, 4, lists, tile_edges, feature_pieces)
    with jax.named_scope("sum_along_x"):
        received_a = exchange(pieces_a, COL, shift_x)
        received_b = exchange(after(pieces_b, received_a[1]), COL, shift_x)
    by_z_a, by_z_b = split_by_z(received_a), split_by_z(received_b)
    act_a, aggregate_a, dpreact_a, dscaled_a = finish_nodes(by_z_a, parts[0])
    from_z_a = gather_z(dscaled_a)
    gathered_a = gather_x(from_z_a)
    act_b, aggregate_b, dpreact_b, dscaled_b = finish_nodes(
        by_z_b, parts[1], from_z_a, gathered_a[1], gathered_a[3]
    )
    from_z_b = gather_z(dscaled_b)
    aggregate = jnp.concatenate([aggregate_a, aggregate_b])
    dpreact = jnp.concatenate([dpreact_a, dpreact_b])
    features, aggregate = after((features, aggregate), dscaled_b)
    with jax.named_scope("weight_grads"):
        grads = jnp.concatenate(
            [
                jnp.einsum("nf,ng->fg", features, dpreact, preferred_element_type=F32),
                jnp.einsum("nf,ng->fg", aggregate, dpreact, preferred_element_type=F32),
            ]
        )
    from_z_b = after(from_z_b, gathered_a)
    gathered_b = gather_x(from_z_b)
    with jax.named_scope("weight_grads"):
        grads = halve(after(grads, from_z_b), ROW, 8, y >> 1)
        grads = halve(grads, ROW, 4, y & 1)
        grads = grads + swap(grads, ROW, 1)
        grads = grads + swap(grads, COL, 4)
    sums_a = [
        products(2 + side, 1, lists, tile_edges, gathered_a, raw=True)[0] for side in (1, 0)
    ]
    gathered_b = after(gathered_b, sums_a, grads)
    with jax.named_scope("weight_grads"):
        grads = after(grads, gathered_b)
        grads = grads + swap(grads, COL, 8)
    [for_other] = products(5, 1, lists, tile_edges, gathered_b, first=sums_a[0])
    from_other = lax.ppermute(for_other, ROW, SWAP_CORE)
    with jax.named_scope("weight_grads"):
        grads = after(grads, for_other)
        along_x = swap(grads, COL, 1)
    [own] = products(4, 1, lists, tile_edges, gathered_b, first=sums_a[1])
    half = own.shape[0] // 2
    with jax.named_scope("sum_early"):
        both = add_up([own[:half], from_other[:half]])
        size = half // 4
        by_y = [both[:size]] + [both[k * size : (k + 1) * size].astype(BF16) for k in (1, 2, 3)]
        received = exchange(by_y, ROW, shift_y)
        along_y = add_up(received)
        size //= 2
        early = along_y[:size] + lax.ppermute(along_y[size:].astype(BF16), ROW, SWAP_Z).astype(F32)
    with jax.named_scope("sum_late"):
        both = add_up([own[half:], from_other[half:]])
        across_z = both[: half // 2] + lax.ppermute(
            both[half // 2 :].astype(BF16), ROW, SWAP_Z
        ).astype(F32)
        by_y = [across_z[:size]]
        by_y += [across_z[k * size : (k + 1) * size].astype(BF16) for k in (1, 2, 3)]
        late = add_up(exchange(by_y, ROW, shift_y))
    neighbour_grad = jnp.concatenate([early, late])
    with jax.named_scope("weight_grads"):
        grads = grads + after(along_x, received[1])
        grads = grads + swap(grads, COL, 2)
        grads = grads + swap(grads, ROW, 2)
        grads = join(after(grads, along_y), ROW, 4, y & 1)
        grads = join(grads, ROW, 8, y >> 1)
    own_grad = jnp.einsum("ng,fg->nf", dpreact, w_self, preferred_element_type=F32)
    feature_grad = (own_grad + neighbour_grad).astype(BF16)
    total_nodes = nodes * lax.axis_size(ROW) * lax.axis_size(COL)
    grads = grads * (1.0 / math.sqrt(total_nodes))
    return jnp.concatenate([act_a, act_b]), feature_grad, grads[:width], grads[width:]


def solution(mesh):
    by_device = P((ROW, COL))
    return jax.shard_map(
        per_device,
        mesh=mesh,
        in_specs=(
            P((ROW, COL), None),
            P(),
            P(),
            P((ROW, COL), None),
            by_device,
            by_device,
            by_device,
            P(None, (ROW, COL), None),
            by_device,
        ),
        out_specs=(P((ROW, COL), None), P((ROW, COL), None), P(), P()),
        check_vma=False,
    )
```

```python
import functools
import math

import jax
import jax.numpy as jnp
from jax import lax
from jax.experimental import pallas as pl
from jax.experimental.pallas import tpu as pltpu
from jax.sharding import PartitionSpec as P

F32, BF16, I32 = jnp.float32, jnp.bfloat16, jnp.int32
ROW, COL = "row", "col"
UNROLL = 8
FORWARD_VMEM, BACKWARD_VMEM = 56 << 20, 32 << 20


def shift_x(k):
    return [(4 * z + x, 4 * z + (x + k) % 4) for z in range(4) for x in range(4)]


def shift_z(k):
    return [(4 * z + x, 4 * ((z + k) % 4) + x) for z in range(4) for x in range(4)]


def shift_y(k):
    return [(4 * y + i, 4 * ((y + k) % 4) + i) for y in range(4) for i in range(4)]


SWAP_Z = [(i, i ^ 2) for i in range(16)]
SWAP_CORE = [(i, i ^ 1) for i in range(16)]


LISTS = 6


def list_kernel(pos, count, rows, cols, slot, src, dst, counts):
    stretch = slot.shape[0] // LISTS
    x, z, y, zl, core = pos[0], pos[1], pos[2], pos[3], pos[4]
    for i in range(LISTS):
        counts[i] = 0

    def place(s, _):
        row, col = rows[s], cols[s]
        tile, chunk = row & 1, (row >> 1) & 1
        rx, rz = (row >> 2) & 3, row >> 4
        ccore, czl, cy = (col >> 2) & 1, (col >> 3) & 1, col >> 4
        other = ccore ^ core
        half = (czl ^ zl) * 4 + (col & 3)
        n = counts[chunk]
        counts[chunk] = n + 1
        at = chunk * stretch + n
        slot[at] = s
        src[at] = other * 32 + ((y - cy) & 3) * 8 + half
        dst[at] = ((rx - x) & 3) * 8 + ((rz - z) & 3) * 2 + tile
        which = 2 + 2 * chunk + other
        n = counts[which]
        counts[which] = n + 1
        at = which * stretch + n
        slot[at] = s
        src[at] = ((x - rx) & 3) * 8 + ((z - rz) & 3) * 2 + tile
        ky, kz, low = (cy - y) & 3, czl ^ zl, col & 1
        late = (col >> 1) & 1
        dst[at] = jnp.where(late == 0, ky * 4 + kz * 2 + low, 16 + kz * 8 + ky * 2 + low)
        return 0

    lax.fori_loop(0, count[0], place, 0)
    for i in range(LISTS):
        end = i * stretch + counts[i]
        for u in range(UNROLL):
            slot[end + u] = 0
            src[end + u] = 0
            dst[end + u] = 32


def make_lists(pos, count, rows, cols):
    smem = pl.BlockSpec(memory_space=pltpu.SMEM)
    length = LISTS * (rows.shape[0] + UNROLL)
    return pl.pallas_call(
        list_kernel,
        out_shape=[jax.ShapeDtypeStruct((length,), I32)] * 3 + [jax.ShapeDtypeStruct((8,), I32)],
        in_specs=[smem] * 4,
        out_specs=[smem] * 4,
        name="slot_lists",
    )(pos, count, rows, cols)


def edge_tile(edges, s):
    edge_count, _, tile = edges.shape
    column = lax.broadcasted_iota(I32, (tile, tile), 0).astype(F32).astype(BF16)
    one, zero = jnp.ones((tile, tile), BF16), jnp.zeros((tile, tile), BF16)
    total = None
    for k in range(edge_count):
        edge = jnp.broadcast_to(edges[k, pl.ds(s, 1), :], (16, tile)).astype(F32).astype(BF16)
        match = jnp.where(jnp.concatenate([edge] * (tile // 16), axis=0) == column, one, zero)
        total = match if total is None else total + match
    return total


def product_kernel(which, n_in, n_out, carried, raw, counts, slot, src, dst, edges, *refs):
    ins, refs = refs[:n_in], refs[n_in:]
    first, refs = (refs[0], refs[1:]) if carried else (None, refs)
    outs, refs = refs[:n_out], refs[n_out:]
    held, total, staged, in_sems, out_sems = refs
    tile, width = edges.shape[2], held.shape[1]
    n = counts[which]
    base = which * (src.shape[0] // LISTS)
    copies, at = [], 0
    for i, ref in enumerate(ins):
        size = ref.shape[0]
        copies.append(pltpu.make_async_copy(ref, held.at[pl.ds(at, size)], in_sems.at[i]))
        at += size
    results = total.shape[0] - tile
    if carried:
        copies.append(pltpu.make_async_copy(first, total.at[pl.ds(0, results)], in_sems.at[n_in]))
    for copy in copies:
        copy.start()
    if not carried:

        @pl.loop(0, results // tile)
        def _(i):
            total[pl.ds(pl.multiple_of(i * tile, tile), tile), :] = jnp.zeros((tile, width), F32)

    for copy in copies:
        copy.wait()
    over = ((0,), (0,)) if which < 2 else ((1,), (0,))

    @pl.loop(0, (n + UNROLL - 1) // UNROLL)
    def _(i):
        for half in range(0, UNROLL, 4):
            at = [base + i * UNROLL + half + u for u in range(4)]
            parts = [
                lax.dot_general(
                    edge_tile(edges, slot[p]),
                    held[pl.ds(pl.multiple_of(src[p] * tile, tile), tile), :],
                    (over, ((), ())),
                    preferred_element_type=F32,
                )
                for p in at
            ]
            for p, part in zip(at, parts):
                total[pl.ds(pl.multiple_of(dst[p] * tile, tile), tile), :] += part

    rows = results // n_out
    sends = []
    for o, ref in enumerate(outs):
        if raw:
            source = total.at[pl.ds(o * rows, rows)]
        else:
            source = staged.at[pl.ds(o * rows, rows)]

            @pl.loop(0, rows // tile)
            def _(i, o=o):
                part = pl.ds(pl.multiple_of(o * rows + i * tile, tile), tile)
                staged[part, :] = total[part, :].astype(BF16)

        sends.append(pltpu.make_async_copy(source, ref, out_sems.at[o]))
        sends[-1].start()
    for send in sends:
        send.wait()


def products(which, n_out, lists, edges, pieces, first=None, raw=False):
    slot, src, dst, counts = lists
    tile, width = edges.shape[2], pieces[0].shape[1]
    n_in, rows = len(pieces), sum(p.shape[0] for p in pieces)
    carried = first is not None
    smem, anywhere = pl.BlockSpec(memory_space=pltpu.SMEM), pl.BlockSpec(memory_space=pl.ANY)
    return pl.pallas_call(
        functools.partial(product_kernel, which, n_in, n_out, carried, raw),
        out_shape=[jax.ShapeDtypeStruct((32 * tile // n_out, width), F32 if raw else BF16)] * n_out,
        in_specs=[smem] * 4 + [pl.BlockSpec(memory_space=pltpu.VMEM)] + [anywhere] * (n_in + carried),
        out_specs=[anywhere] * n_out,
        scratch_shapes=[
            pltpu.VMEM((rows, width), BF16),
            pltpu.VMEM((33 * tile, width), F32),
            pltpu.VMEM((16, 128) if raw else (32 * tile, width), BF16),
            pltpu.SemaphoreType.DMA((n_in + 1,)),
            pltpu.SemaphoreType.DMA((n_out,)),
        ],
        compiler_params=pltpu.CompilerParams(
            vmem_limit_bytes=FORWARD_VMEM if which < 2 else BACKWARD_VMEM
        ),
        cost_estimate=pl.CostEstimate(
            flops=128 * tile * tile * width * 2 * 4, bytes_accessed=12 << 20, transcendentals=0
        ),
        name="tile_products",
    )(counts, slot, src, dst, edges, *pieces, *([first] if carried else []))


def spread(value, axis, shift):
    return [lax.ppermute(value, axis, shift(k)) for k in (1, 2, 3)]


def exchange(pieces, axis, shift):
    return [pieces[0]] + [lax.ppermute(pieces[k], axis, shift(k)) for k in (1, 2, 3)]


def add_up(parts):
    total = parts[0].astype(F32)
    for part in parts[1:]:
        total = total + part.astype(F32)
    return total


def after(value, *events):
    return lax.optimization_barrier((value, events))[0]


def swap(value, axis, bit):
    return lax.ppermute(value, axis, [(i, i ^ bit) for i in range(16)])


def scatter_sum(value, index, axis, shift):
    size = value.shape[0] // 4
    pieces = [lax.dynamic_slice_in_dim(value, ((index + k) & 3) * size, size) for k in range(4)]
    return add_up(exchange(pieces, axis, shift))


def gather_back(value, index, axis, shift):
    size = value.shape[0]
    full = jnp.zeros((4 * size, value.shape[1]), value.dtype)
    for k, piece in enumerate([value] + spread(value, axis, shift)):
        full = lax.dynamic_update_slice_in_dim(full, piece, ((index - k) & 3) * size, 0)
    return full


def node_part(features, cotangent, degree_wide, neighbour_sum, w_self, w_neigh):
    aggregate = (neighbour_sum / degree_wide).astype(BF16)
    preact = jnp.dot(features, w_self, preferred_element_type=F32) + jnp.dot(
        aggregate, w_neigh, preferred_element_type=F32
    )
    gate = jax.nn.sigmoid(preact)
    activations = (preact * gate).astype(BF16)
    slope = gate * (1.0 + preact * (1.0 - gate))
    dpreact = (cotangent.astype(F32) * slope).astype(BF16)
    dscaled = (
        jnp.einsum("ng,fg->nf", dpreact, w_neigh, preferred_element_type=F32) / degree_wide
    ).astype(BF16)
    return activations, aggregate, dpreact, dscaled


def per_device(
    features, w_self, w_neigh, cotangent, degree, tile_rows, tile_cols, tile_edges, tile_count
):
    nodes, width = features.shape
    row, col = lax.axis_index(ROW), lax.axis_index(COL)
    x, z, y = col & 3, col >> 2, row >> 2
    pos = jnp.stack([x, z, y, (row >> 1) & 1, row & 1]).astype(I32)

    with jax.named_scope("gather_features"):
        across = lax.ppermute(features, ROW, SWAP_Z)
        near = [features, across]
        for k in (1, 2, 3):
            near += [lax.ppermute(p, ROW, shift_y(k)) for p in (features, across)]
    lists = make_lists(pos, tile_count, tile_rows, tile_cols)
    near = after(near, lists)
    with jax.named_scope("gather_features"):
        feature_pieces = near + [lax.ppermute(p, ROW, SWAP_CORE) for p in near]

    degree_wide = degree.astype(F32)[:, None]
    parts = [slice(0, nodes // 2), slice(nodes // 2, nodes)]

    def split_by_z(received):
        with jax.named_scope("sum_along_x"):
            along_x = add_up(received)
            rounded = along_x.astype(BF16)
            size = along_x.shape[0] // 4
            return [along_x[:size]] + [rounded[k * size : (k + 1) * size] for k in (1, 2, 3)]

    def finish_nodes(by_z, mine, *events):
        with jax.named_scope("sum_along_z"):
            neighbour_sum = add_up(after(exchange(by_z, COL, shift_z), *events))
        return node_part(
            features[mine], cotangent[mine], degree_wide[mine], neighbour_sum, w_self, w_neigh
        )

    def gather_z(dscaled):
        with jax.named_scope("gather_dscaled"):
            return [dscaled] + spread(dscaled, COL, shift_z)

    def gather_x(from_z):
        with jax.named_scope("gather_dscaled"):
            line = jnp.concatenate(from_z)
            return [line] + spread(line, COL, shift_x)

    pieces_a = products(0, 4, lists, tile_edges, feature_pieces)
    lists, features, cotangent, degree_wide = after(
        (lists, features, cotangent, degree_wide), pieces_a
    )
    pieces_b = products(1, 4, lists, tile_edges, feature_pieces)
    with jax.named_scope("sum_along_x"):
        received_a = exchange(pieces_a, COL, shift_x)
        received_b = exchange(after(pieces_b, received_a[1]), COL, shift_x)
    by_z_a, by_z_b = split_by_z(received_a), split_by_z(received_b)
    act_a, aggregate_a, dpreact_a, dscaled_a = finish_nodes(by_z_a, parts[0])
    from_z_a = gather_z(dscaled_a)
    gathered_a = gather_x(from_z_a)
    act_b, aggregate_b, dpreact_b, dscaled_b = finish_nodes(
        by_z_b, parts[1], from_z_a, gathered_a[1], gathered_a[3]
    )
    from_z_b = gather_z(dscaled_b)
    aggregate = jnp.concatenate([aggregate_a, aggregate_b])
    dpreact = jnp.concatenate([dpreact_a, dpreact_b])
    features, aggregate = after((features, aggregate), dscaled_b)
    with jax.named_scope("weight_grads"):
        grads = jnp.concatenate(
            [
                jnp.einsum("nf,ng->fg", features, dpreact, preferred_element_type=F32),
                jnp.einsum("nf,ng->fg", aggregate, dpreact, preferred_element_type=F32),
            ]
        )
    gathered_b = gather_x(after(from_z_b, gathered_a))
    sums_a = [
        products(2 + side, 1, lists, tile_edges, gathered_a, raw=True)[0] for side in (1, 0)
    ]
    gathered_b = after(gathered_b, sums_a, grads)
    with jax.named_scope("weight_grads"):
        grads = scatter_sum(after(grads, gathered_b), y, ROW, shift_y)
    [for_other] = products(5, 1, lists, tile_edges, gathered_b, first=sums_a[0])
    from_other = lax.ppermute(for_other, ROW, SWAP_CORE)
    with jax.named_scope("weight_grads"):
        grads = after(grads, for_other)
        along_x = spread(grads, COL, shift_x)
    [own] = products(4, 1, lists, tile_edges, gathered_b, first=sums_a[1])
    half = own.shape[0] // 2
    with jax.named_scope("sum_early"):
        both = add_up([own[:half], from_other[:half]])
        size = half // 4
        by_y = [both[:size]] + [both[k * size : (k + 1) * size].astype(BF16) for k in (1, 2, 3)]
        received = exchange(by_y, ROW, shift_y)
        along_y = add_up(received)
        size //= 2
        early = along_y[:size] + lax.ppermute(along_y[size:].astype(BF16), ROW, SWAP_Z).astype(F32)
    with jax.named_scope("sum_late"):
        both = add_up([own[half:], from_other[half:]])
        across_z = both[: half // 2] + lax.ppermute(
            both[half // 2 :].astype(BF16), ROW, SWAP_Z
        ).astype(F32)
        by_y = [across_z[:size]]
        by_y += [across_z[k * size : (k + 1) * size].astype(BF16) for k in (1, 2, 3)]
        late = add_up(exchange(by_y, ROW, shift_y))
    neighbour_grad = jnp.concatenate([early, late])
    with jax.named_scope("weight_grads"):
        grads = add_up([grads] + after(along_x, own))
        grads = grads + after(swap(grads, COL, 4), received[1])
        grads = grads + swap(grads, COL, 8)
        grads = grads + swap(grads, ROW, 1)
        grads = grads + swap(grads, ROW, 2)
        grads = gather_back(grads, y, ROW, shift_y)
    own_grad = jnp.einsum("ng,fg->nf", dpreact, w_self, preferred_element_type=F32)
    feature_grad = (own_grad + neighbour_grad).astype(BF16)
    total_nodes = nodes * lax.axis_size(ROW) * lax.axis_size(COL)
    grads = grads * (1.0 / math.sqrt(total_nodes))
    return jnp.concatenate([act_a, act_b]), feature_grad, grads[:width], grads[width:]


def solution(mesh):
    by_device = P((ROW, COL))
    return jax.shard_map(
        per_device,
        mesh=mesh,
        in_specs=(
            P((ROW, COL), None),
            P(),
            P(),
            P((ROW, COL), None),
            by_device,
            by_device,
            by_device,
            P(None, (ROW, COL), None),
            by_device,
        ),
        out_specs=(P((ROW, COL), None), P((ROW, COL), None), P(), P()),
        check_vma=False,
    )
```

```python
import functools
import math

import jax
import jax.numpy as jnp
from jax import lax
from jax.experimental import pallas as pl
from jax.experimental.pallas import tpu as pltpu
from jax.sharding import PartitionSpec as P

F32, BF16, I32 = jnp.float32, jnp.bfloat16, jnp.int32
ROW, COL = "row", "col"
UNROLL = 8
FORWARD_VMEM, BACKWARD_VMEM = 56 << 20, 32 << 20


def shift_x(k):
    return [(4 * z + x, 4 * z + (x + k) % 4) for z in range(4) for x in range(4)]


def shift_z(k):
    return [(4 * z + x, 4 * ((z + k) % 4) + x) for z in range(4) for x in range(4)]


def shift_y(k):
    return [(4 * y + i, 4 * ((y + k) % 4) + i) for y in range(4) for i in range(4)]


SWAP_Z = [(i, i ^ 2) for i in range(16)]
SWAP_CORE = [(i, i ^ 1) for i in range(16)]


LISTS = 6


def list_kernel(pos, count, rows, cols, slot, src, dst, counts):
    stretch = slot.shape[0] // LISTS
    x, z, y, zl, core = pos[0], pos[1], pos[2], pos[3], pos[4]
    for i in range(LISTS):
        counts[i] = 0

    def place(s, _):
        row, col = rows[s], cols[s]
        tile, chunk = row & 1, (row >> 1) & 1
        rx, rz = (row >> 2) & 3, row >> 4
        ccore, czl, cy = (col >> 2) & 1, (col >> 3) & 1, col >> 4
        other = ccore ^ core
        half = (czl ^ zl) * 4 + (col & 3)
        n = counts[chunk]
        counts[chunk] = n + 1
        at = chunk * stretch + n
        slot[at] = s
        src[at] = other * 32 + ((y - cy) & 3) * 8 + half
        dst[at] = ((rx - x) & 3) * 8 + ((rz - z) & 3) * 2 + tile
        which = 2 + 2 * chunk + other
        n = counts[which]
        counts[which] = n + 1
        at = which * stretch + n
        slot[at] = s
        src[at] = ((x - rx) & 3) * 8 + ((z - rz) & 3) * 2 + tile
        ky, kz, low = (cy - y) & 3, czl ^ zl, col & 1
        late = (col >> 1) & 1
        dst[at] = jnp.where(late == 0, ky * 4 + kz * 2 + low, 16 + kz * 8 + ky * 2 + low)
        return 0

    lax.fori_loop(0, count[0], place, 0)
    for i in range(LISTS):
        end = i * stretch + counts[i]
        for u in range(UNROLL):
            slot[end + u] = 0
            src[end + u] = 0
            dst[end + u] = 32


def make_lists(pos, count, rows, cols):
    smem = pl.BlockSpec(memory_space=pltpu.SMEM)
    length = LISTS * (rows.shape[0] + UNROLL)
    return pl.pallas_call(
        list_kernel,
        out_shape=[jax.ShapeDtypeStruct((length,), I32)] * 3 + [jax.ShapeDtypeStruct((8,), I32)],
        in_specs=[smem] * 4,
        out_specs=[smem] * 4,
        name="slot_lists",
    )(pos, count, rows, cols)


def edge_tile(edges, s):
    edge_count, _, tile = edges.shape
    column = lax.broadcasted_iota(I32, (tile, tile), 0).astype(F32).astype(BF16)
    one, zero = jnp.ones((tile, tile), BF16), jnp.zeros((tile, tile), BF16)
    total = None
    for k in range(edge_count):
        edge = jnp.broadcast_to(edges[k, pl.ds(s, 1), :], (16, tile)).astype(F32).astype(BF16)
        match = jnp.where(jnp.concatenate([edge] * (tile // 16), axis=0) == column, one, zero)
        total = match if total is None else total + match
    return total


def product_kernel(which, n_in, n_out, carried, raw, counts, slot, src, dst, edges, *refs):
    ins, refs = refs[:n_in], refs[n_in:]
    first, refs = (refs[0], refs[1:]) if carried else (None, refs)
    outs, refs = refs[:n_out], refs[n_out:]
    held, total, staged, in_sems, out_sems = refs
    tile, width = edges.shape[2], held.shape[1]
    n = counts[which]
    base = which * (src.shape[0] // LISTS)
    copies, at = [], 0
    for i, ref in enumerate(ins):
        size = ref.shape[0]
        copies.append(pltpu.make_async_copy(ref, held.at[pl.ds(at, size)], in_sems.at[i]))
        at += size
    results = total.shape[0] - tile
    if carried:
        copies.append(pltpu.make_async_copy(first, total.at[pl.ds(0, results)], in_sems.at[n_in]))
    for copy in copies:
        copy.start()
    if not carried:

        @pl.loop(0, results // tile)
        def _(i):
            total[pl.ds(pl.multiple_of(i * tile, tile), tile), :] = jnp.zeros((tile, width), F32)

    for copy in copies:
        copy.wait()
    over = ((0,), (0,)) if which < 2 else ((1,), (0,))

    @pl.loop(0, (n + UNROLL - 1) // UNROLL)
    def _(i):
        for half in range(0, UNROLL, 4):
            at = [base + i * UNROLL + half + u for u in range(4)]
            parts = [
                lax.dot_general(
                    edge_tile(edges, slot[p]),
                    held[pl.ds(pl.multiple_of(src[p] * tile, tile), tile), :],
                    (over, ((), ())),
                    preferred_element_type=F32,
                )
                for p in at
            ]
            for p, part in zip(at, parts):
                total[pl.ds(pl.multiple_of(dst[p] * tile, tile), tile), :] += part

    rows = results // n_out
    sends = []
    for o, ref in enumerate(outs):
        if raw:
            source = total.at[pl.ds(o * rows, rows)]
        else:
            source = staged.at[pl.ds(o * rows, rows)]

            @pl.loop(0, rows // tile)
            def _(i, o=o):
                part = pl.ds(pl.multiple_of(o * rows + i * tile, tile), tile)
                staged[part, :] = total[part, :].astype(BF16)

        sends.append(pltpu.make_async_copy(source, ref, out_sems.at[o]))
        sends[-1].start()
    for send in sends:
        send.wait()


def products(which, n_out, lists, edges, pieces, first=None, raw=False):
    slot, src, dst, counts = lists
    tile, width = edges.shape[2], pieces[0].shape[1]
    n_in, rows = len(pieces), sum(p.shape[0] for p in pieces)
    carried = first is not None
    smem, anywhere = pl.BlockSpec(memory_space=pltpu.SMEM), pl.BlockSpec(memory_space=pl.ANY)
    return pl.pallas_call(
        functools.partial(product_kernel, which, n_in, n_out, carried, raw),
        out_shape=[jax.ShapeDtypeStruct((32 * tile // n_out, width), F32 if raw else BF16)] * n_out,
        in_specs=[smem] * 4 + [pl.BlockSpec(memory_space=pltpu.VMEM)] + [anywhere] * (n_in + carried),
        out_specs=[anywhere] * n_out,
        scratch_shapes=[
            pltpu.VMEM((rows, width), BF16),
            pltpu.VMEM((33 * tile, width), F32),
            pltpu.VMEM((16, 128) if raw else (32 * tile, width), BF16),
            pltpu.SemaphoreType.DMA((n_in + 1,)),
            pltpu.SemaphoreType.DMA((n_out,)),
        ],
        compiler_params=pltpu.CompilerParams(
            vmem_limit_bytes=FORWARD_VMEM if which < 2 else BACKWARD_VMEM
        ),
        cost_estimate=pl.CostEstimate(
            flops=128 * tile * tile * width * 2 * 4, bytes_accessed=12 << 20, transcendentals=0
        ),
        name="tile_products",
    )(counts, slot, src, dst, edges, *pieces, *([first] if carried else []))


def spread(value, axis, shift):
    return [lax.ppermute(value, axis, shift(k)) for k in (1, 2, 3)]


def exchange(pieces, axis, shift):
    return [pieces[0]] + [lax.ppermute(pieces[k], axis, shift(k)) for k in (1, 2, 3)]


def add_up(parts):
    total = parts[0].astype(F32)
    for part in parts[1:]:
        total = total + part.astype(F32)
    return total


def after(value, *events):
    return lax.optimization_barrier((value, events))[0]


def swap(value, axis, bit):
    return lax.ppermute(value, axis, [(i, i ^ bit) for i in range(16)])


def halve(value, axis, bit, set_here):
    size = value.shape[0] // 2
    kept = lax.dynamic_slice_in_dim(value, set_here * size, size)
    return kept + swap(lax.dynamic_slice_in_dim(value, (1 - set_here) * size, size), axis, bit)


def gather_back(value, index, axis, shift):
    size = value.shape[0]
    full = jnp.zeros((4 * size, value.shape[1]), value.dtype)
    for k, piece in enumerate([value] + spread(value, axis, shift)):
        full = lax.dynamic_update_slice_in_dim(full, piece, ((index - k) & 3) * size, 0)
    return full


def node_part(features, cotangent, degree_wide, neighbour_sum, w_self, w_neigh):
    aggregate = (neighbour_sum / degree_wide).astype(BF16)
    preact = jnp.dot(features, w_self, preferred_element_type=F32) + jnp.dot(
        aggregate, w_neigh, preferred_element_type=F32
    )
    gate = jax.nn.sigmoid(preact)
    activations = (preact * gate).astype(BF16)
    slope = gate * (1.0 + preact * (1.0 - gate))
    dpreact = (cotangent.astype(F32) * slope).astype(BF16)
    dscaled = (
        jnp.einsum("ng,fg->nf", dpreact, w_neigh, preferred_element_type=F32) / degree_wide
    ).astype(BF16)
    return activations, aggregate, dpreact, dscaled


def per_device(
    features, w_self, w_neigh, cotangent, degree, tile_rows, tile_cols, tile_edges, tile_count
):
    nodes, width = features.shape
    row, col = lax.axis_index(ROW), lax.axis_index(COL)
    x, z, y = col & 3, col >> 2, row >> 2
    pos = jnp.stack([x, z, y, (row >> 1) & 1, row & 1]).astype(I32)

    with jax.named_scope("gather_features"):
        across = lax.ppermute(features, ROW, SWAP_Z)
        near = [features, across]
        for k in (1, 2, 3):
            near += [lax.ppermute(p, ROW, shift_y(k)) for p in (features, across)]
    lists = make_lists(pos, tile_count, tile_rows, tile_cols)
    near = after(near, lists)
    with jax.named_scope("gather_features"):
        feature_pieces = near + [lax.ppermute(p, ROW, SWAP_CORE) for p in near]

    degree_wide = degree.astype(F32)[:, None]
    parts = [slice(0, nodes // 2), slice(nodes // 2, nodes)]

    def split_by_z(received):
        with jax.named_scope("sum_along_x"):
            along_x = add_up(received)
            rounded = along_x.astype(BF16)
            size = along_x.shape[0] // 4
            return [along_x[:size]] + [rounded[k * size : (k + 1) * size] for k in (1, 2, 3)]

    def finish_nodes(by_z, mine, *events):
        with jax.named_scope("sum_along_z"):
            neighbour_sum = add_up(after(exchange(by_z, COL, shift_z), *events))
        return node_part(
            features[mine], cotangent[mine], degree_wide[mine], neighbour_sum, w_self, w_neigh
        )

    def gather_z(dscaled):
        with jax.named_scope("gather_dscaled"):
            return [dscaled] + spread(dscaled, COL, shift_z)

    def gather_x(from_z):
        with jax.named_scope("gather_dscaled"):
            line = jnp.concatenate(from_z)
            return [line] + spread(line, COL, shift_x)

    pieces_a = products(0, 4, lists, tile_edges, feature_pieces)
    lists, features, cotangent, degree_wide = after(
        (lists, features, cotangent, degree_wide), pieces_a
    )
    pieces_b = products(1, 4, lists, tile_edges, feature_pieces)
    with jax.named_scope("sum_along_x"):
        received_a = exchange(pieces_a, COL, shift_x)
        received_b = exchange(after(pieces_b, received_a[1]), COL, shift_x)
    by_z_a, by_z_b = split_by_z(received_a), split_by_z(received_b)
    act_a, aggregate_a, dpreact_a, dscaled_a = finish_nodes(by_z_a, parts[0])
    from_z_a = gather_z(dscaled_a)
    gathered_a = gather_x(from_z_a)
    act_b, aggregate_b, dpreact_b, dscaled_b = finish_nodes(
        by_z_b, parts[1], from_z_a, gathered_a[1], gathered_a[3]
    )
    from_z_b = gather_z(dscaled_b)
    aggregate = jnp.concatenate([aggregate_a, aggregate_b])
    dpreact = jnp.concatenate([dpreact_a, dpreact_b])
    features, aggregate = after((features, aggregate), dscaled_b)
    with jax.named_scope("weight_grads"):
        grads = jnp.concatenate(
            [
                jnp.einsum("nf,ng->fg", features, dpreact, preferred_element_type=F32),
                jnp.einsum("nf,ng->fg", aggregate, dpreact, preferred_element_type=F32),
            ]
        )
    from_z_b = after(from_z_b, gathered_a)
    gathered_b = gather_x(from_z_b)
    with jax.named_scope("weight_grads"):
        grads = halve(after(grads, from_z_b), ROW, 8, y >> 1)
        grads = halve(grads, ROW, 4, y & 1)
    sums_a = [
        products(2 + side, 1, lists, tile_edges, gathered_a, raw=True)[0] for side in (1, 0)
    ]
    gathered_b = after(gathered_b, sums_a, grads)
    [for_other] = products(5, 1, lists, tile_edges, gathered_b, first=sums_a[0])
    from_other = lax.ppermute(for_other, ROW, SWAP_CORE)
    with jax.named_scope("weight_grads"):
        grads = after(grads, for_other)
        sibling = swap(grads, ROW, 1)
    [own] = products(4, 1, lists, tile_edges, gathered_b, first=sums_a[1])
    half = own.shape[0] // 2
    with jax.named_scope("sum_early"):
        both = add_up([own[:half], from_other[:half]])
        size = half // 4
        by_y = [both[:size]] + [both[k * size : (k + 1) * size].astype(BF16) for k in (1, 2, 3)]
        received = exchange(by_y, ROW, shift_y)
        along_y = add_up(received)
        size //= 2
        early = along_y[:size] + lax.ppermute(along_y[size:].astype(BF16), ROW, SWAP_Z).astype(F32)
    with jax.named_scope("sum_late"):
        both = add_up([own[half:], from_other[half:]])
        across_z = both[: half // 2] + lax.ppermute(
            both[half // 2 :].astype(BF16), ROW, SWAP_Z
        ).astype(F32)
        by_y = [across_z[:size]]
        by_y += [across_z[k * size : (k + 1) * size].astype(BF16) for k in (1, 2, 3)]
        late = add_up(exchange(by_y, ROW, shift_y))
    neighbour_grad = jnp.concatenate([early, late])
    with jax.named_scope("weight_grads"):
        grads = grads + after(sibling, own)
        grads = grads + after(swap(grads, COL, 4), received[1])
        for bit in (8, 1, 2):
            grads = grads + swap(grads, COL, bit)
        grads = grads + swap(grads, ROW, 2)
        grads = gather_back(grads, y, ROW, shift_y)
    own_grad = jnp.einsum("ng,fg->nf", dpreact, w_self, preferred_element_type=F32)
    feature_grad = (own_grad + neighbour_grad).astype(BF16)
    total_nodes = nodes * lax.axis_size(ROW) * lax.axis_size(COL)
    grads = grads * (1.0 / math.sqrt(total_nodes))
    return jnp.concatenate([act_a, act_b]), feature_grad, grads[:width], grads[width:]


def solution(mesh):
    by_device = P((ROW, COL))
    return jax.shard_map(
        per_device,
        mesh=mesh,
        in_specs=(
            P((ROW, COL), None),
            P(),
            P(),
            P((ROW, COL), None),
            by_device,
            by_device,
            by_device,
            P(None, (ROW, COL), None),
            by_device,
        ),
        out_specs=(P((ROW, COL), None), P((ROW, COL), None), P(), P()),
        check_vma=False,
    )
```

```python
import functools
import math

import jax
import jax.numpy as jnp
from jax import lax
from jax.experimental import pallas as pl
from jax.experimental.pallas import tpu as pltpu
from jax.sharding import PartitionSpec as P

F32, BF16, I32 = jnp.float32, jnp.bfloat16, jnp.int32
ROW, COL = "row", "col"
UNROLL = 8
FORWARD_VMEM, BACKWARD_VMEM = 56 << 20, 32 << 20


def shift_x(k):
    return [(4 * z + x, 4 * z + (x + k) % 4) for z in range(4) for x in range(4)]


def shift_z(k):
    return [(4 * z + x, 4 * ((z + k) % 4) + x) for z in range(4) for x in range(4)]


def shift_y(k):
    return [(4 * y + i, 4 * ((y + k) % 4) + i) for y in range(4) for i in range(4)]


SWAP_Z = [(i, i ^ 2) for i in range(16)]
SWAP_CORE = [(i, i ^ 1) for i in range(16)]


LISTS = 6


def list_kernel(pos, count, rows, cols, slot, src, dst, counts):
    stretch = slot.shape[0] // LISTS
    x, z, y, zl, core = pos[0], pos[1], pos[2], pos[3], pos[4]
    for i in range(LISTS):
        counts[i] = 0

    def place(s, _):
        row, col = rows[s], cols[s]
        tile, chunk = row & 1, (row >> 1) & 1
        rx, rz = (row >> 2) & 3, row >> 4
        ccore, czl, cy = (col >> 2) & 1, (col >> 3) & 1, col >> 4
        other = ccore ^ core
        half = (czl ^ zl) * 4 + (col & 3)
        n = counts[chunk]
        counts[chunk] = n + 1
        at = chunk * stretch + n
        slot[at] = s
        src[at] = other * 32 + ((y - cy) & 3) * 8 + half
        dst[at] = ((rx - x) & 3) * 8 + ((rz - z) & 3) * 2 + tile
        which = 2 + 2 * chunk + other
        n = counts[which]
        counts[which] = n + 1
        at = which * stretch + n
        slot[at] = s
        src[at] = ((x - rx) & 3) * 8 + ((z - rz) & 3) * 2 + tile
        ky, kz, low = (cy - y) & 3, czl ^ zl, col & 1
        late = (col >> 1) & 1
        dst[at] = jnp.where(late == 0, ky * 4 + kz * 2 + low, 16 + kz * 8 + ky * 2 + low)
        return 0

    lax.fori_loop(0, count[0], place, 0)
    for i in range(LISTS):
        end = i * stretch + counts[i]
        for u in range(UNROLL):
            slot[end + u] = 0
            src[end + u] = 0
            dst[end + u] = 32


def make_lists(pos, count, rows, cols):
    smem = pl.BlockSpec(memory_space=pltpu.SMEM)
    length = LISTS * (rows.shape[0] + UNROLL)
    return pl.pallas_call(
        list_kernel,
        out_shape=[jax.ShapeDtypeStruct((length,), I32)] * 3 + [jax.ShapeDtypeStruct((8,), I32)],
        in_specs=[smem] * 4,
        out_specs=[smem] * 4,
        name="slot_lists",
    )(pos, count, rows, cols)


def edge_tile(edges, s):
    edge_count, _, tile = edges.shape
    column = lax.broadcasted_iota(I32, (tile, tile), 0).astype(F32).astype(BF16)
    one, zero = jnp.ones((tile, tile), BF16), jnp.zeros((tile, tile), BF16)
    total = None
    for k in range(edge_count):
        edge = jnp.broadcast_to(edges[k, pl.ds(s, 1), :], (16, tile)).astype(F32).astype(BF16)
        match = jnp.where(jnp.concatenate([edge] * (tile // 16), axis=0) == column, one, zero)
        total = match if total is None else total + match
    return total


def product_kernel(which, n_in, n_out, carried, raw, counts, slot, src, dst, edges, *refs):
    ins, refs = refs[:n_in], refs[n_in:]
    first, refs = (refs[0], refs[1:]) if carried else (None, refs)
    outs, refs = refs[:n_out], refs[n_out:]
    held, total, staged, in_sems, out_sems = refs
    tile, width = edges.shape[2], held.shape[1]
    n = counts[which]
    base = which * (src.shape[0] // LISTS)
    copies, at = [], 0
    for i, ref in enumerate(ins):
        size = ref.shape[0]
        copies.append(pltpu.make_async_copy(ref, held.at[pl.ds(at, size)], in_sems.at[i]))
        at += size
    results = total.shape[0] - tile
    if carried:
        copies.append(pltpu.make_async_copy(first, total.at[pl.ds(0, results)], in_sems.at[n_in]))
    for copy in copies:
        copy.start()
    if not carried:

        @pl.loop(0, results // tile)
        def _(i):
            total[pl.ds(pl.multiple_of(i * tile, tile), tile), :] = jnp.zeros((tile, width), F32)

    for copy in copies:
        copy.wait()
    over = ((0,), (0,)) if which < 2 else ((1,), (0,))

    @pl.loop(0, (n + UNROLL - 1) // UNROLL)
    def _(i):
        for half in range(0, UNROLL, 4):
            at = [base + i * UNROLL + half + u for u in range(4)]
            parts = [
                lax.dot_general(
                    edge_tile(edges, slot[p]),
                    held[pl.ds(pl.multiple_of(src[p] * tile, tile), tile), :],
                    (over, ((), ())),
                    preferred_element_type=F32,
                )
                for p in at
            ]
            for p, part in zip(at, parts):
                total[pl.ds(pl.multiple_of(dst[p] * tile, tile), tile), :] += part

    rows = results // n_out
    sends = []
    for o, ref in enumerate(outs):
        if raw:
            source = total.at[pl.ds(o * rows, rows)]
        else:
            source = staged.at[pl.ds(o * rows, rows)]

            @pl.loop(0, rows // tile)
            def _(i, o=o):
                part = pl.ds(pl.multiple_of(o * rows + i * tile, tile), tile)
                staged[part, :] = total[part, :].astype(BF16)

        sends.append(pltpu.make_async_copy(source, ref, out_sems.at[o]))
        sends[-1].start()
    for send in sends:
        send.wait()


def products(which, n_out, lists, edges, pieces, first=None, raw=False):
    slot, src, dst, counts = lists
    tile, width = edges.shape[2], pieces[0].shape[1]
    n_in, rows = len(pieces), sum(p.shape[0] for p in pieces)
    carried = first is not None
    smem, anywhere = pl.BlockSpec(memory_space=pltpu.SMEM), pl.BlockSpec(memory_space=pl.ANY)
    return pl.pallas_call(
        functools.partial(product_kernel, which, n_in, n_out, carried, raw),
        out_shape=[jax.ShapeDtypeStruct((32 * tile // n_out, width), F32 if raw else BF16)] * n_out,
        in_specs=[smem] * 4 + [pl.BlockSpec(memory_space=pltpu.VMEM)] + [anywhere] * (n_in + carried),
        out_specs=[anywhere] * n_out,
        scratch_shapes=[
            pltpu.VMEM((rows, width), BF16),
            pltpu.VMEM((33 * tile, width), F32),
            pltpu.VMEM((16, 128) if raw else (32 * tile, width), BF16),
            pltpu.SemaphoreType.DMA((n_in + 1,)),
            pltpu.SemaphoreType.DMA((n_out,)),
        ],
        compiler_params=pltpu.CompilerParams(
            vmem_limit_bytes=FORWARD_VMEM if which < 2 else BACKWARD_VMEM
        ),
        cost_estimate=pl.CostEstimate(
            flops=128 * tile * tile * width * 2 * 4, bytes_accessed=12 << 20, transcendentals=0
        ),
        name="tile_products",
    )(counts, slot, src, dst, edges, *pieces, *([first] if carried else []))


def spread(value, axis, shift):
    return [lax.ppermute(value, axis, shift(k)) for k in (1, 2, 3)]


def exchange(pieces, axis, shift):
    return [pieces[0]] + [lax.ppermute(pieces[k], axis, shift(k)) for k in (1, 2, 3)]


def add_up(parts):
    total = parts[0].astype(F32)
    for part in parts[1:]:
        total = total + part.astype(F32)
    return total


def after(value, *events):
    return lax.optimization_barrier((value, events))[0]


def swap(value, axis, bit):
    return lax.ppermute(value, axis, [(i, i ^ bit) for i in range(16)])


def halve(value, axis, bit, set_here):
    size = value.shape[0] // 2
    kept = lax.dynamic_slice_in_dim(value, set_here * size, size)
    return kept + swap(lax.dynamic_slice_in_dim(value, (1 - set_here) * size, size), axis, bit)


def gather_back(value, index, axis, shift):
    size = value.shape[0]
    full = jnp.zeros((4 * size, value.shape[1]), value.dtype)
    for k, piece in enumerate([value] + spread(value, axis, shift)):
        full = lax.dynamic_update_slice_in_dim(full, piece, ((index - k) & 3) * size, 0)
    return full


def node_part(features, cotangent, degree_wide, neighbour_sum, w_self, w_neigh):
    aggregate = (neighbour_sum / degree_wide).astype(BF16)
    preact = jnp.dot(features, w_self, preferred_element_type=F32) + jnp.dot(
        aggregate, w_neigh, preferred_element_type=F32
    )
    gate = jax.nn.sigmoid(preact)
    activations = (preact * gate).astype(BF16)
    slope = gate * (1.0 + preact * (1.0 - gate))
    dpreact = (cotangent.astype(F32) * slope).astype(BF16)
    dscaled = (
        jnp.einsum("ng,fg->nf", dpreact, w_neigh, preferred_element_type=F32) / degree_wide
    ).astype(BF16)
    return activations, aggregate, dpreact, dscaled


def per_device(
    features, w_self, w_neigh, cotangent, degree, tile_rows, tile_cols, tile_edges, tile_count
):
    nodes, width = features.shape
    row, col = lax.axis_index(ROW), lax.axis_index(COL)
    x, z, y = col & 3, col >> 2, row >> 2
    pos = jnp.stack([x, z, y, (row >> 1) & 1, row & 1]).astype(I32)

    with jax.named_scope("gather_features"):
        across = lax.ppermute(features, ROW, SWAP_Z)
        near = [features, across]
        for k in (1, 2, 3):
            near += [lax.ppermute(p, ROW, shift_y(k)) for p in (features, across)]
    lists = make_lists(pos, tile_count, tile_rows, tile_cols)
    near = after(near, lists)
    with jax.named_scope("gather_features"):
        feature_pieces = near + [lax.ppermute(p, ROW, SWAP_CORE) for p in near]

    degree_wide = degree.astype(F32)[:, None]
    parts = [slice(0, nodes // 2), slice(nodes // 2, nodes)]

    def split_by_z(received):
        with jax.named_scope("sum_along_x"):
            along_x = add_up(received)
            rounded = along_x.astype(BF16)
            size = along_x.shape[0] // 4
            return [along_x[:size]] + [rounded[k * size : (k + 1) * size] for k in (1, 2, 3)]

    def finish_nodes(by_z, mine, *events):
        with jax.named_scope("sum_along_z"):
            neighbour_sum = add_up(after(exchange(by_z, COL, shift_z), *events))
        return node_part(
            features[mine], cotangent[mine], degree_wide[mine], neighbour_sum, w_self, w_neigh
        )

    def gather_z(dscaled):
        with jax.named_scope("gather_dscaled"):
            return [dscaled] + spread(dscaled, COL, shift_z)

    def gather_x(from_z):
        with jax.named_scope("gather_dscaled"):
            line = jnp.concatenate(from_z)
            return [line] + spread(line, COL, shift_x)

    pieces_a = products(0, 4, lists, tile_edges, feature_pieces)
    lists, features, cotangent, degree_wide = after(
        (lists, features, cotangent, degree_wide), pieces_a
    )
    pieces_b = products(1, 4, lists, tile_edges, feature_pieces)
    with jax.named_scope("sum_along_x"):
        received_a = exchange(pieces_a, COL, shift_x)
        received_b = exchange(after(pieces_b, received_a[1]), COL, shift_x)
    by_z_a, by_z_b = split_by_z(received_a), split_by_z(received_b)
    act_a, aggregate_a, dpreact_a, dscaled_a = finish_nodes(by_z_a, parts[0])
    from_z_a = gather_z(dscaled_a)
    gathered_a = gather_x(from_z_a)
    act_b, aggregate_b, dpreact_b, dscaled_b = finish_nodes(
        by_z_b, parts[1], from_z_a, gathered_a[1], gathered_a[3]
    )
    from_z_b = gather_z(dscaled_b)
    aggregate = jnp.concatenate([aggregate_a, aggregate_b])
    dpreact = jnp.concatenate([dpreact_a, dpreact_b])
    features, aggregate = after((features, aggregate), dscaled_b)
    with jax.named_scope("weight_grads"):
        grads = jnp.concatenate(
            [
                jnp.einsum("nf,ng->fg", features, dpreact, preferred_element_type=F32),
                jnp.einsum("nf,ng->fg", aggregate, dpreact, preferred_element_type=F32),
            ]
        )
    from_z_b = after(from_z_b, gathered_a)
    gathered_b = gather_x(from_z_b)
    with jax.named_scope("weight_grads"):
        grads = halve(after(grads, from_z_b), ROW, 8, y >> 1)
        grads = halve(grads, ROW, 4, y & 1)
    sums_a = [
        products(2 + side, 1, lists, tile_edges, gathered_a, raw=True)[0] for side in (1, 0)
    ]
    gathered_b = after(gathered_b, sums_a, grads)
    with jax.named_scope("weight_grads"):
        grads = after(grads, gathered_b)
        grads = grads + swap(grads, ROW, 1)
    [for_other] = products(5, 1, lists, tile_edges, gathered_b, first=sums_a[0])
    from_other = lax.ppermute(for_other, ROW, SWAP_CORE)
    with jax.named_scope("weight_grads"):
        grads = after(grads, for_other)
        across = swap(grads, ROW, 2)
    [own] = products(4, 1, lists, tile_edges, gathered_b, first=sums_a[1])
    half = own.shape[0] // 2
    with jax.named_scope("sum_early"):
        both = add_up([own[:half], from_other[:half]])
        size = half // 4
        by_y = [both[:size]] + [both[k * size : (k + 1) * size].astype(BF16) for k in (1, 2, 3)]
        received = exchange(by_y, ROW, shift_y)
        along_y = add_up(received)
        size //= 2
        early = along_y[:size] + lax.ppermute(along_y[size:].astype(BF16), ROW, SWAP_Z).astype(F32)
    with jax.named_scope("sum_late"):
        both = add_up([own[half:], from_other[half:]])
        across_z = both[: half // 2] + lax.ppermute(
            both[half // 2 :].astype(BF16), ROW, SWAP_Z
        ).astype(F32)
        by_y = [across_z[:size]]
        by_y += [across_z[k * size : (k + 1) * size].astype(BF16) for k in (1, 2, 3)]
        late = add_up(exchange(by_y, ROW, shift_y))
    neighbour_grad = jnp.concatenate([early, late])
    with jax.named_scope("weight_grads"):
        grads = grads + after(across, own)
        grads = grads + after(swap(grads, COL, 1), received[1])
        for bit in (2, 4, 8):
            grads = grads + swap(grads, COL, bit)
        grads = gather_back(grads, y, ROW, shift_y)
    own_grad = jnp.einsum("ng,fg->nf", dpreact, w_self, preferred_element_type=F32)
    feature_grad = (own_grad + neighbour_grad).astype(BF16)
    total_nodes = nodes * lax.axis_size(ROW) * lax.axis_size(COL)
    grads = grads * (1.0 / math.sqrt(total_nodes))
    return jnp.concatenate([act_a, act_b]), feature_grad, grads[:width], grads[width:]


def solution(mesh):
    by_device = P((ROW, COL))
    return jax.shard_map(
        per_device,
        mesh=mesh,
        in_specs=(
            P((ROW, COL), None),
            P(),
            P(),
            P((ROW, COL), None),
            by_device,
            by_device,
            by_device,
            P(None, (ROW, COL), None),
            by_device,
        ),
        out_specs=(P((ROW, COL), None), P((ROW, COL), None), P(), P()),
        check_vma=False,
    )
```

```python
import functools
import math

import jax
import jax.numpy as jnp
from jax import lax
from jax.experimental import pallas as pl
from jax.experimental.pallas import tpu as pltpu
from jax.sharding import PartitionSpec as P

F32, BF16, I32 = jnp.float32, jnp.bfloat16, jnp.int32
ROW, COL = "row", "col"
UNROLL = 8
FORWARD_VMEM, BACKWARD_VMEM = 56 << 20, 32 << 20


def shift_x(k):
    return [(4 * z + x, 4 * z + (x + k) % 4) for z in range(4) for x in range(4)]


def shift_z(k):
    return [(4 * z + x, 4 * ((z + k) % 4) + x) for z in range(4) for x in range(4)]


def shift_y(k):
    return [(4 * y + i, 4 * ((y + k) % 4) + i) for y in range(4) for i in range(4)]


SWAP_Z = [(i, i ^ 2) for i in range(16)]
SWAP_CORE = [(i, i ^ 1) for i in range(16)]


LISTS = 6


def list_kernel(pos, count, rows, cols, slot, src, dst, counts):
    stretch = slot.shape[0] // LISTS
    x, z, y, zl, core = pos[0], pos[1], pos[2], pos[3], pos[4]
    for i in range(LISTS):
        counts[i] = 0

    def place(s, _):
        row, col = rows[s], cols[s]
        tile, chunk = row & 1, (row >> 1) & 1
        rx, rz = (row >> 2) & 3, row >> 4
        ccore, czl, cy = (col >> 2) & 1, (col >> 3) & 1, col >> 4
        other = ccore ^ core
        half = (czl ^ zl) * 4 + (col & 3)
        n = counts[chunk]
        counts[chunk] = n + 1
        at = chunk * stretch + n
        slot[at] = s
        src[at] = other * 32 + ((y - cy) & 3) * 8 + half
        dst[at] = ((rx - x) & 3) * 8 + ((rz - z) & 3) * 2 + tile
        which = 2 + 2 * chunk + other
        n = counts[which]
        counts[which] = n + 1
        at = which * stretch + n
        slot[at] = s
        src[at] = ((x - rx) & 3) * 8 + ((z - rz) & 3) * 2 + tile
        ky, kz, low = (cy - y) & 3, czl ^ zl, col & 1
        late = (col >> 1) & 1
        dst[at] = jnp.where(late == 0, ky * 4 + kz * 2 + low, 16 + kz * 8 + ky * 2 + low)
        return 0

    lax.fori_loop(0, count[0], place, 0)
    for i in range(LISTS):
        end = i * stretch + counts[i]
        for u in range(UNROLL):
            slot[end + u] = 0
            src[end + u] = 0
            dst[end + u] = 32


def make_lists(pos, count, rows, cols):
    smem = pl.BlockSpec(memory_space=pltpu.SMEM)
    length = LISTS * (rows.shape[0] + UNROLL)
    return pl.pallas_call(
        list_kernel,
        out_shape=[jax.ShapeDtypeStruct((length,), I32)] * 3 + [jax.ShapeDtypeStruct((8,), I32)],
        in_specs=[smem] * 4,
        out_specs=[smem] * 4,
        name="slot_lists",
    )(pos, count, rows, cols)


def edge_tile(edges, s):
    edge_count, _, tile = edges.shape
    column = lax.broadcasted_iota(I32, (tile, tile), 0).astype(F32).astype(BF16)
    one, zero = jnp.ones((tile, tile), BF16), jnp.zeros((tile, tile), BF16)
    total = None
    for k in range(edge_count):
        edge = jnp.broadcast_to(edges[k, pl.ds(s, 1), :], (16, tile)).astype(F32).astype(BF16)
        match = jnp.where(jnp.concatenate([edge] * (tile // 16), axis=0) == column, one, zero)
        total = match if total is None else total + match
    return total


def product_kernel(which, n_in, n_out, carried, raw, counts, slot, src, dst, edges, *refs):
    ins, refs = refs[:n_in], refs[n_in:]
    first, refs = (refs[0], refs[1:]) if carried else (None, refs)
    outs, refs = refs[:n_out], refs[n_out:]
    held, total, staged, in_sems, out_sems = refs
    tile, width = edges.shape[2], held.shape[1]
    n = counts[which]
    base = which * (src.shape[0] // LISTS)
    copies, at = [], 0
    for i, ref in enumerate(ins):
        size = ref.shape[0]
        copies.append(pltpu.make_async_copy(ref, held.at[pl.ds(at, size)], in_sems.at[i]))
        at += size
    results = total.shape[0] - tile
    if carried:
        copies.append(pltpu.make_async_copy(first, total.at[pl.ds(0, results)], in_sems.at[n_in]))
    for copy in copies:
        copy.start()
    if not carried:

        @pl.loop(0, results // tile)
        def _(i):
            total[pl.ds(pl.multiple_of(i * tile, tile), tile), :] = jnp.zeros((tile, width), F32)

    for copy in copies:
        copy.wait()
    over = ((0,), (0,)) if which < 2 else ((1,), (0,))

    @pl.loop(0, (n + UNROLL - 1) // UNROLL)
    def _(i):
        for half in range(0, UNROLL, 4):
            at = [base + i * UNROLL + half + u for u in range(4)]
            parts = [
                lax.dot_general(
                    edge_tile(edges, slot[p]),
                    held[pl.ds(pl.multiple_of(src[p] * tile, tile), tile), :],
                    (over, ((), ())),
                    preferred_element_type=F32,
                )
                for p in at
            ]
            for p, part in zip(at, parts):
                total[pl.ds(pl.multiple_of(dst[p] * tile, tile), tile), :] += part

    rows = results // n_out
    sends = []
    for o, ref in enumerate(outs):
        if raw:
            source = total.at[pl.ds(o * rows, rows)]
        else:
            source = staged.at[pl.ds(o * rows, rows)]

            @pl.loop(0, rows // tile)
            def _(i, o=o):
                part = pl.ds(pl.multiple_of(o * rows + i * tile, tile), tile)
                staged[part, :] = total[part, :].astype(BF16)

        sends.append(pltpu.make_async_copy(source, ref, out_sems.at[o]))
        sends[-1].start()
    for send in sends:
        send.wait()


def products(which, n_out, lists, edges, pieces, first=None, raw=False):
    slot, src, dst, counts = lists
    tile, width = edges.shape[2], pieces[0].shape[1]
    n_in, rows = len(pieces), sum(p.shape[0] for p in pieces)
    carried = first is not None
    smem, anywhere = pl.BlockSpec(memory_space=pltpu.SMEM), pl.BlockSpec(memory_space=pl.ANY)
    return pl.pallas_call(
        functools.partial(product_kernel, which, n_in, n_out, carried, raw),
        out_shape=[jax.ShapeDtypeStruct((32 * tile // n_out, width), F32 if raw else BF16)] * n_out,
        in_specs=[smem] * 4 + [pl.BlockSpec(memory_space=pltpu.VMEM)] + [anywhere] * (n_in + carried),
        out_specs=[anywhere] * n_out,
        scratch_shapes=[
            pltpu.VMEM((rows, width), BF16),
            pltpu.VMEM((33 * tile, width), F32),
            pltpu.VMEM((16, 128) if raw else (32 * tile, width), BF16),
            pltpu.SemaphoreType.DMA((n_in + 1,)),
            pltpu.SemaphoreType.DMA((n_out,)),
        ],
        compiler_params=pltpu.CompilerParams(
            vmem_limit_bytes=FORWARD_VMEM if which < 2 else BACKWARD_VMEM
        ),
        cost_estimate=pl.CostEstimate(
            flops=128 * tile * tile * width * 2 * 4, bytes_accessed=12 << 20, transcendentals=0
        ),
        name="tile_products",
    )(counts, slot, src, dst, edges, *pieces, *([first] if carried else []))


def spread(value, axis, shift):
    return [lax.ppermute(value, axis, shift(k)) for k in (1, 2, 3)]


def exchange(pieces, axis, shift):
    return [pieces[0]] + [lax.ppermute(pieces[k], axis, shift(k)) for k in (1, 2, 3)]


def add_up(parts):
    total = parts[0].astype(F32)
    for part in parts[1:]:
        total = total + part.astype(F32)
    return total


def after(value, *events):
    return lax.optimization_barrier((value, events))[0]


def swap(value, axis, bit):
    return lax.ppermute(value, axis, [(i, i ^ bit) for i in range(16)])


def halve(value, axis, bit, set_here):
    size = value.shape[0] // 2
    kept = lax.dynamic_slice_in_dim(value, set_here * size, size)
    return kept + swap(lax.dynamic_slice_in_dim(value, (1 - set_here) * size, size), axis, bit)


def gather_back(value, index, axis, shift):
    size = value.shape[0]
    full = jnp.zeros((4 * size, value.shape[1]), value.dtype)
    for k, piece in enumerate([value] + spread(value, axis, shift)):
        full = lax.dynamic_update_slice_in_dim(full, piece, ((index - k) & 3) * size, 0)
    return full


def node_part(features, cotangent, degree_wide, neighbour_sum, w_self, w_neigh):
    aggregate = (neighbour_sum / degree_wide).astype(BF16)
    preact = jnp.dot(features, w_self, preferred_element_type=F32) + jnp.dot(
        aggregate, w_neigh, preferred_element_type=F32
    )
    gate = jax.nn.sigmoid(preact)
    activations = (preact * gate).astype(BF16)
    slope = gate * (1.0 + preact * (1.0 - gate))
    dpreact = (cotangent.astype(F32) * slope).astype(BF16)
    dscaled = (
        jnp.einsum("ng,fg->nf", dpreact, w_neigh, preferred_element_type=F32) / degree_wide
    ).astype(BF16)
    return activations, aggregate, dpreact, dscaled


def per_device(
    features, w_self, w_neigh, cotangent, degree, tile_rows, tile_cols, tile_edges, tile_count
):
    nodes, width = features.shape
    row, col = lax.axis_index(ROW), lax.axis_index(COL)
    x, z, y = col & 3, col >> 2, row >> 2
    pos = jnp.stack([x, z, y, (row >> 1) & 1, row & 1]).astype(I32)

    with jax.named_scope("gather_features"):
        across = lax.ppermute(features, ROW, SWAP_Z)
        near = [features, across]
        for k in (1, 2, 3):
            near += [lax.ppermute(p, ROW, shift_y(k)) for p in (features, across)]
    lists = make_lists(pos, tile_count, tile_rows, tile_cols)
    near = after(near, lists)
    with jax.named_scope("gather_features"):
        feature_pieces = near + [lax.ppermute(p, ROW, SWAP_CORE) for p in near]

    degree_wide = degree.astype(F32)[:, None]
    parts = [slice(0, nodes // 2), slice(nodes // 2, nodes)]

    def split_by_z(received):
        with jax.named_scope("sum_along_x"):
            along_x = add_up(received)
            rounded = along_x.astype(BF16)
            size = along_x.shape[0] // 4
            return [along_x[:size]] + [rounded[k * size : (k + 1) * size] for k in (1, 2, 3)]

    def finish_nodes(by_z, mine, *events):
        with jax.named_scope("sum_along_z"):
            neighbour_sum = add_up(after(exchange(by_z, COL, shift_z), *events))
        return node_part(
            features[mine], cotangent[mine], degree_wide[mine], neighbour_sum, w_self, w_neigh
        )

    def gather_z(dscaled):
        with jax.named_scope("gather_dscaled"):
            return [dscaled] + spread(dscaled, COL, shift_z)

    def gather_x(from_z):
        with jax.named_scope("gather_dscaled"):
            line = jnp.concatenate(from_z)
            return [line] + spread(line, COL, shift_x)

    pieces_a = products(0, 4, lists, tile_edges, feature_pieces)
    lists, features, cotangent, degree_wide = after(
        (lists, features, cotangent, degree_wide), pieces_a
    )
    with jax.named_scope("sum_along_x"):
        received_a = exchange(pieces_a, COL, shift_x)
    pieces_b = products(1, 4, lists, tile_edges, feature_pieces)
    with jax.named_scope("sum_along_x"):
        received_b = exchange(pieces_b, COL, shift_x)
    by_z_a, by_z_b = split_by_z(received_a), split_by_z(received_b)
    act_a, aggregate_a, dpreact_a, dscaled_a = finish_nodes(by_z_a, parts[0])
    from_z_a = gather_z(dscaled_a)
    gathered_a = gather_x(from_z_a)
    act_b, aggregate_b, dpreact_b, dscaled_b = finish_nodes(
        by_z_b, parts[1], from_z_a, gathered_a[1], gathered_a[3]
    )
    from_z_b = gather_z(dscaled_b)
    aggregate = jnp.concatenate([aggregate_a, aggregate_b])
    dpreact = jnp.concatenate([dpreact_a, dpreact_b])
    features, aggregate = after((features, aggregate), dscaled_b)
    with jax.named_scope("weight_grads"):
        grads = jnp.concatenate(
            [
                jnp.einsum("nf,ng->fg", features, dpreact, preferred_element_type=F32),
                jnp.einsum("nf,ng->fg", aggregate, dpreact, preferred_element_type=F32),
            ]
        )
    from_z_b = after(from_z_b, gathered_a)
    gathered_b = gather_x(from_z_b)
    with jax.named_scope("weight_grads"):
        grads = halve(after(grads, from_z_b), ROW, 8, y >> 1)
        grads = halve(grads, ROW, 4, y & 1)
    sums_a = [
        products(2 + side, 1, lists, tile_edges, gathered_a, raw=True)[0] for side in (1, 0)
    ]
    gathered_b = after(gathered_b, sums_a, grads)
    with jax.named_scope("weight_grads"):
        grads = after(grads, gathered_b)
        grads = grads + swap(grads, ROW, 1)
    [for_other] = products(5, 1, lists, tile_edges, gathered_b, first=sums_a[0])
    from_other = lax.ppermute(for_other, ROW, SWAP_CORE)
    with jax.named_scope("weight_grads"):
        grads = after(grads, for_other)
        across = swap(grads, ROW, 2)
    [own] = products(4, 1, lists, tile_edges, gathered_b, first=sums_a[1])
    half = own.shape[0] // 2
    with jax.named_scope("sum_early"):
        both = add_up([own[:half], from_other[:half]])
        size = half // 4
        by_y = [both[:size]] + [both[k * size : (k + 1) * size].astype(BF16) for k in (1, 2, 3)]
        received = exchange(by_y, ROW, shift_y)
        along_y = add_up(received)
        size //= 2
        early = along_y[:size] + lax.ppermute(along_y[size:].astype(BF16), ROW, SWAP_Z).astype(F32)
    with jax.named_scope("sum_late"):
        both = add_up([own[half:], from_other[half:]])
        across_z = both[: half // 2] + lax.ppermute(
            both[half // 2 :].astype(BF16), ROW, SWAP_Z
        ).astype(F32)
        by_y = [across_z[:size]]
        by_y += [across_z[k * size : (k + 1) * size].astype(BF16) for k in (1, 2, 3)]
        late = add_up(exchange(by_y, ROW, shift_y))
    neighbour_grad = jnp.concatenate([early, late])
    with jax.named_scope("weight_grads"):
        grads = grads + after(across, own)
        grads = grads + after(swap(grads, COL, 1), received[1])
        for bit in (2, 4, 8):
            grads = grads + swap(grads, COL, bit)
        grads = gather_back(grads, y, ROW, shift_y)
    own_grad = jnp.einsum("ng,fg->nf", dpreact, w_self, preferred_element_type=F32)
    feature_grad = (own_grad + neighbour_grad).astype(BF16)
    total_nodes = nodes * lax.axis_size(ROW) * lax.axis_size(COL)
    grads = grads * (1.0 / math.sqrt(total_nodes))
    return jnp.concatenate([act_a, act_b]), feature_grad, grads[:width], grads[width:]


def solution(mesh):
    by_device = P((ROW, COL))
    return jax.shard_map(
        per_device,
        mesh=mesh,
        in_specs=(
            P((ROW, COL), None),
            P(),
            P(),
            P((ROW, COL), None),
            by_device,
            by_device,
            by_device,
            P(None, (ROW, COL), None),
            by_device,
        ),
        out_specs=(P((ROW, COL), None), P((ROW, COL), None), P(), P()),
        check_vma=False,
    )
```

```python
import functools
import math

import jax
import jax.numpy as jnp
from jax import lax
from jax.experimental import pallas as pl
from jax.experimental.pallas import tpu as pltpu
from jax.sharding import PartitionSpec as P

F32, BF16, I32 = jnp.float32, jnp.bfloat16, jnp.int32
ROW, COL = "row", "col"
UNROLL = 8
FORWARD_VMEM, BACKWARD_VMEM = 56 << 20, 32 << 20


def shift_x(k):
    return [(4 * z + x, 4 * z + (x + k) % 4) for z in range(4) for x in range(4)]


def shift_z(k):
    return [(4 * z + x, 4 * ((z + k) % 4) + x) for z in range(4) for x in range(4)]


def shift_y(k):
    return [(4 * y + i, 4 * ((y + k) % 4) + i) for y in range(4) for i in range(4)]


SWAP_Z = [(i, i ^ 2) for i in range(16)]
SWAP_CORE = [(i, i ^ 1) for i in range(16)]


LISTS = 6


def list_kernel(pos, count, rows, cols, slot, src, dst, counts):
    stretch = slot.shape[0] // LISTS
    x, z, y, zl, core = pos[0], pos[1], pos[2], pos[3], pos[4]
    for i in range(LISTS):
        counts[i] = 0

    def place(s, _):
        row, col = rows[s], cols[s]
        tile, chunk = row & 1, (row >> 1) & 1
        rx, rz = (row >> 2) & 3, row >> 4
        ccore, czl, cy = (col >> 2) & 1, (col >> 3) & 1, col >> 4
        other = ccore ^ core
        half = (czl ^ zl) * 4 + (col & 3)
        n = counts[chunk]
        counts[chunk] = n + 1
        at = chunk * stretch + n
        slot[at] = s
        src[at] = other * 32 + ((y - cy) & 3) * 8 + half
        dst[at] = ((rx - x) & 3) * 8 + ((rz - z) & 3) * 2 + tile
        which = 2 + 2 * chunk + other
        n = counts[which]
        counts[which] = n + 1
        at = which * stretch + n
        slot[at] = s
        src[at] = ((x - rx) & 3) * 8 + ((z - rz) & 3) * 2 + tile
        ky, kz, low = (cy - y) & 3, czl ^ zl, col & 1
        late = (col >> 1) & 1
        dst[at] = jnp.where(late == 0, ky * 4 + kz * 2 + low, 16 + kz * 8 + ky * 2 + low)
        return 0

    lax.fori_loop(0, count[0], place, 0)
    for i in range(LISTS):
        end = i * stretch + counts[i]
        for u in range(UNROLL):
            slot[end + u] = 0
            src[end + u] = 0
            dst[end + u] = 32


def make_lists(pos, count, rows, cols):
    smem = pl.BlockSpec(memory_space=pltpu.SMEM)
    length = LISTS * (rows.shape[0] + UNROLL)
    return pl.pallas_call(
        list_kernel,
        out_shape=[jax.ShapeDtypeStruct((length,), I32)] * 3 + [jax.ShapeDtypeStruct((8,), I32)],
        in_specs=[smem] * 4,
        out_specs=[smem] * 4,
        name="slot_lists",
    )(pos, count, rows, cols)


def edge_tile(edges, s):
    edge_count, _, tile = edges.shape
    column = lax.broadcasted_iota(I32, (tile, tile), 0).astype(F32).astype(BF16)
    one, zero = jnp.ones((tile, tile), BF16), jnp.zeros((tile, tile), BF16)
    total = None
    for k in range(edge_count):
        edge = jnp.broadcast_to(edges[k, pl.ds(s, 1), :], (16, tile)).astype(F32).astype(BF16)
        match = jnp.where(jnp.concatenate([edge] * (tile // 16), axis=0) == column, one, zero)
        total = match if total is None else total + match
    return total


def product_kernel(which, n_in, n_out, carried, raw, counts, slot, src, dst, edges, *refs):
    ins, refs = refs[:n_in], refs[n_in:]
    first, refs = (refs[0], refs[1:]) if carried else (None, refs)
    outs, refs = refs[:n_out], refs[n_out:]
    held, total, staged, in_sems, out_sems = refs
    tile, width = edges.shape[2], held.shape[1]
    n = counts[which]
    base = which * (src.shape[0] // LISTS)
    copies, at = [], 0
    for i, ref in enumerate(ins):
        size = ref.shape[0]
        copies.append(pltpu.make_async_copy(ref, held.at[pl.ds(at, size)], in_sems.at[i]))
        at += size
    results = total.shape[0] - tile
    if carried:
        copies.append(pltpu.make_async_copy(first, total.at[pl.ds(0, results)], in_sems.at[n_in]))
    for copy in copies:
        copy.start()
    if not carried:

        @pl.loop(0, results // tile)
        def _(i):
            total[pl.ds(pl.multiple_of(i * tile, tile), tile), :] = jnp.zeros((tile, width), F32)

    for copy in copies:
        copy.wait()
    over = ((0,), (0,)) if which < 2 else ((1,), (0,))

    @pl.loop(0, (n + UNROLL - 1) // UNROLL)
    def _(i):
        for half in range(0, UNROLL, 4):
            at = [base + i * UNROLL + half + u for u in range(4)]
            parts = [
                lax.dot_general(
                    edge_tile(edges, slot[p]),
                    held[pl.ds(pl.multiple_of(src[p] * tile, tile), tile), :],
                    (over, ((), ())),
                    preferred_element_type=F32,
                )
                for p in at
            ]
            for p, part in zip(at, parts):
                total[pl.ds(pl.multiple_of(dst[p] * tile, tile), tile), :] += part

    rows = results // n_out
    sends = []
    for o, ref in enumerate(outs):
        if raw:
            source = total.at[pl.ds(o * rows, rows)]
        else:
            source = staged.at[pl.ds(o * rows, rows)]

            @pl.loop(0, rows // tile)
            def _(i, o=o):
                part = pl.ds(pl.multiple_of(o * rows + i * tile, tile), tile)
                staged[part, :] = total[part, :].astype(BF16)

        sends.append(pltpu.make_async_copy(source, ref, out_sems.at[o]))
        sends[-1].start()
    for send in sends:
        send.wait()


def products(which, n_out, lists, edges, pieces, first=None, raw=False):
    slot, src, dst, counts = lists
    tile, width = edges.shape[2], pieces[0].shape[1]
    n_in, rows = len(pieces), sum(p.shape[0] for p in pieces)
    carried = first is not None
    smem, anywhere = pl.BlockSpec(memory_space=pltpu.SMEM), pl.BlockSpec(memory_space=pl.ANY)
    return pl.pallas_call(
        functools.partial(product_kernel, which, n_in, n_out, carried, raw),
        out_shape=[jax.ShapeDtypeStruct((32 * tile // n_out, width), F32 if raw else BF16)] * n_out,
        in_specs=[smem] * 4 + [pl.BlockSpec(memory_space=pltpu.VMEM)] + [anywhere] * (n_in + carried),
        out_specs=[anywhere] * n_out,
        scratch_shapes=[
            pltpu.VMEM((rows, width), BF16),
            pltpu.VMEM((33 * tile, width), F32),
            pltpu.VMEM((16, 128) if raw else (32 * tile, width), BF16),
            pltpu.SemaphoreType.DMA((n_in + 1,)),
            pltpu.SemaphoreType.DMA((n_out,)),
        ],
        compiler_params=pltpu.CompilerParams(
            vmem_limit_bytes=FORWARD_VMEM if which < 2 else BACKWARD_VMEM
        ),
        cost_estimate=pl.CostEstimate(
            flops=128 * tile * tile * width * 2 * 4, bytes_accessed=12 << 20, transcendentals=0
        ),
        name="tile_products",
    )(counts, slot, src, dst, edges, *pieces, *([first] if carried else []))


def spread(value, axis, shift):
    return [lax.ppermute(value, axis, shift(k)) for k in (1, 2, 3)]


def exchange(pieces, axis, shift):
    return [pieces[0]] + [lax.ppermute(pieces[k], axis, shift(k)) for k in (1, 2, 3)]


def add_up(parts):
    total = parts[0].astype(F32)
    for part in parts[1:]:
        total = total + part.astype(F32)
    return total


def after(value, *events):
    return lax.optimization_barrier((value, events))[0]


def swap(value, axis, bit):
    return lax.ppermute(value, axis, [(i, i ^ bit) for i in range(16)])


def halve(value, axis, bit, set_here):
    size = value.shape[0] // 2
    kept = lax.dynamic_slice_in_dim(value, set_here * size, size)
    return kept + swap(lax.dynamic_slice_in_dim(value, (1 - set_here) * size, size), axis, bit)


def gather_back(value, index, axis, shift):
    size = value.shape[0]
    full = jnp.zeros((4 * size, value.shape[1]), value.dtype)
    for k, piece in enumerate([value] + spread(value, axis, shift)):
        full = lax.dynamic_update_slice_in_dim(full, piece, ((index - k) & 3) * size, 0)
    return full


def node_part(features, cotangent, degree_wide, neighbour_sum, w_self, w_neigh):
    aggregate = (neighbour_sum / degree_wide).astype(BF16)
    preact = jnp.dot(features, w_self, preferred_element_type=F32) + jnp.dot(
        aggregate, w_neigh, preferred_element_type=F32
    )
    gate = jax.nn.sigmoid(preact)
    activations = (preact * gate).astype(BF16)
    slope = gate * (1.0 + preact * (1.0 - gate))
    dpreact = (cotangent.astype(F32) * slope).astype(BF16)
    dscaled = (
        jnp.einsum("ng,fg->nf", dpreact, w_neigh, preferred_element_type=F32) / degree_wide
    ).astype(BF16)
    return activations, aggregate, dpreact, dscaled


def per_device(
    features, w_self, w_neigh, cotangent, degree, tile_rows, tile_cols, tile_edges, tile_count
):
    nodes, width = features.shape
    row, col = lax.axis_index(ROW), lax.axis_index(COL)
    x, z, y = col & 3, col >> 2, row >> 2
    pos = jnp.stack([x, z, y, (row >> 1) & 1, row & 1]).astype(I32)

    with jax.named_scope("gather_features"):
        across = lax.ppermute(features, ROW, SWAP_Z)
        near = [features, across]
        for k in (1, 2, 3):
            near += [lax.ppermute(p, ROW, shift_y(k)) for p in (features, across)]
    lists = make_lists(pos, tile_count, tile_rows, tile_cols)
    near = after(near, lists)
    with jax.named_scope("gather_features"):
        feature_pieces = near + [lax.ppermute(p, ROW, SWAP_CORE) for p in near]

    degree_wide = degree.astype(F32)[:, None]
    parts = [slice(0, nodes // 2), slice(nodes // 2, nodes)]

    def split_by_z(received):
        with jax.named_scope("sum_along_x"):
            along_x = add_up(received)
            rounded = along_x.astype(BF16)
            size = along_x.shape[0] // 4
            return [along_x[:size]] + [rounded[k * size : (k + 1) * size] for k in (1, 2, 3)]

    def finish_nodes(by_z, mine, *events):
        with jax.named_scope("sum_along_z"):
            neighbour_sum = add_up(after(exchange(by_z, COL, shift_z), *events))
        return node_part(
            features[mine], cotangent[mine], degree_wide[mine], neighbour_sum, w_self, w_neigh
        )

    def gather_z(dscaled):
        with jax.named_scope("gather_dscaled"):
            return [dscaled] + spread(dscaled, COL, shift_z)

    def gather_x(from_z):
        with jax.named_scope("gather_dscaled"):
            line = jnp.concatenate(from_z)
            return [line] + spread(line, COL, shift_x)

    pieces_a = products(0, 4, lists, tile_edges, feature_pieces)
    lists, features, cotangent, degree_wide = after(
        (lists, features, cotangent, degree_wide), pieces_a
    )
    with jax.named_scope("sum_along_x"):
        received_a = exchange(pieces_a, COL, shift_x)
    pieces_b = products(1, 4, lists, tile_edges, feature_pieces)
    with jax.named_scope("sum_along_x"):
        received_b = exchange(pieces_b, COL, shift_x)
    by_z_a, by_z_b = split_by_z(received_a), split_by_z(received_b)
    act_a, aggregate_a, dpreact_a, dscaled_a = finish_nodes(by_z_a, parts[0])
    from_z_a = gather_z(dscaled_a)
    gathered_a = gather_x(from_z_a)
    act_b, aggregate_b, dpreact_b, dscaled_b = finish_nodes(
        by_z_b, parts[1], from_z_a, gathered_a[1], gathered_a[3]
    )
    from_z_b = gather_z(dscaled_b)
    aggregate = jnp.concatenate([aggregate_a, aggregate_b])
    dpreact = jnp.concatenate([dpreact_a, dpreact_b])
    features, aggregate = after((features, aggregate), dscaled_b)
    with jax.named_scope("weight_grads"):
        grads = jnp.concatenate(
            [
                jnp.einsum("nf,ng->fg", features, dpreact, preferred_element_type=F32),
                jnp.einsum("nf,ng->fg", aggregate, dpreact, preferred_element_type=F32),
            ]
        )
    from_z_b = after(from_z_b, gathered_a)
    gathered_b = gather_x(from_z_b)
    with jax.named_scope("weight_grads"):
        grads = halve(after(grads, from_z_b), ROW, 8, y >> 1)
        grads = halve(grads, ROW, 4, y & 1)
    sums_a = [
        products(2 + side, 1, lists, tile_edges, gathered_a, raw=True)[0] for side in (1, 0)
    ]
    gathered_b = after(gathered_b, sums_a, grads)
    with jax.named_scope("weight_grads"):
        grads = after(grads, gathered_b)
        grads = grads + swap(grads, ROW, 1)
    for_other = products(5, 2, lists, tile_edges, gathered_b, first=sums_a[0])
    from_other = [lax.ppermute(p, ROW, SWAP_CORE) for p in for_other]
    with jax.named_scope("weight_grads"):
        grads = after(grads, for_other)
        across = swap(grads, ROW, 2)
    own = products(4, 2, lists, tile_edges, gathered_b, first=sums_a[1])
    half = own[0].shape[0]
    with jax.named_scope("sum_early"):
        both = add_up([own[0], from_other[0]])
        size = half // 4
        by_y = [both[:size]] + [both[k * size : (k + 1) * size].astype(BF16) for k in (1, 2, 3)]
        received = exchange(by_y, ROW, shift_y)
        along_y = add_up(received)
        size //= 2
        early = along_y[:size] + lax.ppermute(along_y[size:].astype(BF16), ROW, SWAP_Z).astype(F32)
    with jax.named_scope("sum_late"):
        both = add_up([own[1], from_other[1]])
        across_z = both[: half // 2] + lax.ppermute(
            both[half // 2 :].astype(BF16), ROW, SWAP_Z
        ).astype(F32)
        by_y = [across_z[:size]]
        by_y += [across_z[k * size : (k + 1) * size].astype(BF16) for k in (1, 2, 3)]
        late = add_up(exchange(by_y, ROW, shift_y))
    neighbour_grad = jnp.concatenate([early, late])
    with jax.named_scope("weight_grads"):
        grads = grads + after(across, own)
        grads = grads + after(swap(grads, COL, 1), received[1])
        for bit in (2, 4, 8):
            grads = grads + swap(grads, COL, bit)
        grads = gather_back(grads, y, ROW, shift_y)
    own_grad = jnp.einsum("ng,fg->nf", dpreact, w_self, preferred_element_type=F32)
    feature_grad = (own_grad + neighbour_grad).astype(BF16)
    total_nodes = nodes * lax.axis_size(ROW) * lax.axis_size(COL)
    grads = grads * (1.0 / math.sqrt(total_nodes))
    return jnp.concatenate([act_a, act_b]), feature_grad, grads[:width], grads[width:]


def solution(mesh):
    by_device = P((ROW, COL))
    return jax.shard_map(
        per_device,
        mesh=mesh,
        in_specs=(
            P((ROW, COL), None),
            P(),
            P(),
            P((ROW, COL), None),
            by_device,
            by_device,
            by_device,
            P(None, (ROW, COL), None),
            by_device,
        ),
        out_specs=(P((ROW, COL), None), P((ROW, COL), None), P(), P()),
        check_vma=False,
    )
```
